256 devices in a mesh: dp: 16 (over y, x), seq: 16 (over z, core).
Axes of the slice: x: 4, y: 4, z: 8, core: 2. Of those that a mesh axis runs over, the one named last changes fastest.
Arguments:
- query_proj: bfloat16 [16, 3072, 1024], P('dp', 'seq'), may hold values from -6 to 6
- key_proj: bfloat16 [16, 3072, 1024], P('dp', 'seq'), may hold values from -6 to 6
- value_proj: bfloat16 [16, 3072, 1024], P('dp', 'seq'), may hold values from -6 to 6
- cotangent: bfloat16 [16, 3072, 1024], P('dp', 'seq'), may hold values from -6 to 6
- out_weight: bfloat16 [1024, 1024], replicated, may hold values from -0.1875 to 0.1875
- conv_weight: float32 [31, 1024], replicated, may hold values from -1 to 1
- rec_starts: int32 [16, 2], P('dp'), may hold values from 0 to 3064, as said below
Outputs:
- layer_out: bfloat16 [16, 3072, 1024], P('dp', 'seq')
- query_grad: bfloat16 [16, 3072, 1024], P('dp', 'seq')
- key_grad: bfloat16 [16, 3072, 1024], P('dp', 'seq')
- value_grad: bfloat16 [16, 3072, 1024], P('dp', 'seq')
- weight_grad: float32 [1024, 1024], replicated
- conv_grad: float32 [31, 1024], replicated
The draws below stay inside these ranges and needn't reach their ends.
Inputs may be any that keep to these rules, and one draw needn't show every extreme that they name: `rec_starts`: in each group the first start is 0, the starts rise strictly and each is a multiple of 8; a recording runs up to the next start, the last one to frame 3072 - 1.
All inputs are finite; a program needn't handle non-finite values.
Results may differ from the reference program's by a relative error of at most 0.02.
Values may be sent and summed in bfloat16 or wider, within the bound.
A program may use at most 64 MiB of HBM per device.

```python
import jax
import jax.numpy as jnp
from jax import lax

HEADS = 16
HEAD_DIM = 64
KERN = 31
NREC = 2
D = 1024
LAG = 30
GROUPS = 16
SEQLEN = 3072


def pair_draw(key):
    shape = (GROUPS, SEQLEN, D)
    first = jax.random.fold_in(key, 101)
    second = jax.random.fold_in(key, 102)
    queries = jnp.clip(1.6 * jax.random.normal(first, shape, jnp.float32), -6.0, 6.0)
    keys_out = jnp.clip(1.6 * jax.random.normal(second, shape, jnp.float32), -6.0, 6.0)
    return (queries, keys_out)


def draw_query_proj(key, part):
    return pair_draw(key)[0].astype(jnp.bfloat16)


def draw_key_proj(key, part):
    return pair_draw(key)[1].astype(jnp.bfloat16)


def draw_rec_starts(key, part):
    units = SEQLEN // 8

    def one_group(sub):
        order = jax.random.permutation(sub, units - 1) + 1
        cuts = jnp.sort(order[:NREC - 1])
        return jnp.concatenate([jnp.zeros((1,), jnp.int32), (cuts * 8).astype(jnp.int32)])
    starts = jax.vmap(one_group)(jax.random.split(jax.random.fold_in(key, 201), GROUPS))
    forced = jax.random.randint(jax.random.fold_in(key, 202), (), 0, GROUPS)
    group_ids = jnp.arange(GROUPS, dtype=jnp.int32)[:, None]
    column_ids = jnp.arange(NREC, dtype=jnp.int32)[None, :]
    hit = (group_ids == forced) & (column_ids == NREC - 1)
    return jnp.where(hit, jnp.int32(SEQLEN - 8), starts).astype(jnp.int32)


def steps_of(key, dims, shards, smallest, high):
    gain = 1.0
    for axis_at, blocks in shards:
        steps = jax.random.uniform(jax.random.fold_in(jax.random.fold_in(key, 6), axis_at), (blocks,), jnp.float32, smallest / len(shards), high / len(shards))
        gain = gain * jnp.repeat(jnp.exp(steps), dims[axis_at] // blocks).reshape((-1,) + (1,) * (len(dims) - 1 - axis_at))
    return gain


def bell_draw(stream_key, extent, scale, limit, shards=(), kind=jnp.bfloat16):
    values = jax.random.normal(stream_key, extent, jnp.float32) * scale
    if len(shards) > 0:
        values = steps_of(stream_key, extent, shards, -0.22, 0.18) * values
    return jnp.clip(values, min=-limit, max=limit).astype(kind)


def setup_inputs(seed: int = 0) -> dict:
    arg_keys = jax.random.split(jax.random.key(seed), 8)
    return {
        "query_proj": draw_query_proj(jax.random.fold_in(arg_keys[7], 71), 0),
        "key_proj": draw_key_proj(jax.random.fold_in(arg_keys[7], 71), 0),
        "value_proj": bell_draw(arg_keys[2], (GROUPS, SEQLEN, D), 1.0, 6.0, ((0, 16), (1, 16))),
        "cotangent": bell_draw(arg_keys[3], (GROUPS, SEQLEN, D), 1.0, 6.0, ((0, 16), (1, 16))),
        "out_weight": bell_draw(arg_keys[4], (D, D), D ** -0.5, 0.1875),
        "conv_weight": bell_draw(arg_keys[5], (KERN, D), KERN ** -0.5, 1.0, (), jnp.float32),
        "rec_starts": draw_rec_starts(jax.random.fold_in(arg_keys[7], 71), 0),
    }


def record_ids(frames, starts_row, total):
    above = (frames[:, None] >= starts_row[None, :]).astype(jnp.int32)
    labels = jnp.sum(above, axis=1) - 1
    inside = (frames >= 0) & (frames < total)
    return jnp.where(inside, labels, -2).astype(jnp.int32)


def depthwise(padded, labels_pad, labels_out, weights, count):
    total = jnp.zeros((count, padded.shape[1]), jnp.float32)
    for tap in range(weights.shape[0]):
        window = padded[tap:tap + count].astype(jnp.float32)
        same = (labels_pad[tap:tap + count] == labels_out)[:, None]
        total = total + jnp.where(same, weights[tap][None, :] * window, 0.0)
    return total


def transposed(padded, labels_pad, labels_out, weights, count):
    total = jnp.zeros((count, padded.shape[1]), jnp.float32)
    last = weights.shape[0] - 1
    for tap in range(weights.shape[0]):
        offset = last - tap
        window = padded[offset:offset + count].astype(jnp.float32)
        same = (labels_pad[offset:offset + count] == labels_out)[:, None]
        total = total + jnp.where(same, weights[tap][None, :] * window, 0.0)
    return total


def tap_sums(signal, padded, labels_pad, labels_out, taps):
    count = signal.shape[0]
    rows_out = []
    for tap in range(taps):
        window = padded[tap:tap + count].astype(jnp.float32)
        same = (labels_pad[tap:tap + count] == labels_out)[:, None]
        rows_out.append(jnp.sum(jnp.where(same, signal * window, 0.0), axis=0))
    return jnp.stack(rows_out)


def silu_parts(conv):
    gate_value = jax.nn.sigmoid(conv)
    return conv * gate_value, gate_value * (1.0 + conv * (1.0 - gate_value))


def reference(query_proj, key_proj, value_proj, cotangent, out_weight, conv_weight, rec_starts):
    scale = HEAD_DIM ** -0.5
    frames = jnp.arange(SEQLEN, dtype=jnp.int32)
    before_frames = jnp.arange(-LAG, SEQLEN, dtype=jnp.int32)
    after_frames = jnp.arange(0, SEQLEN + LAG, dtype=jnp.int32)

    def split_heads(array):
        return array.reshape(SEQLEN, HEADS, HEAD_DIM).transpose(1, 0, 2)

    def join_heads(array):
        return array.transpose(1, 0, 2).reshape(SEQLEN, D)

    def head_scores(queries, keys, same):
        raw = jnp.dot(queries, keys.T, preferred_element_type=jnp.float32) * scale
        return jnp.where(same, raw, -1e30)

    def forward_group(items):
        queries, keys, values, starts_row = items
        labels = record_ids(frames, starts_row, SEQLEN)
        same = labels[:, None] == labels[None, :]

        def one_head(parts):
            head_q, head_k, head_v = parts
            scores = head_scores(head_q, head_k, same)
            top = jnp.max(scores, axis=1, keepdims=True)
            norm = top + jnp.log(jnp.sum(jnp.exp(scores - top), axis=1, keepdims=True))
            probs = jnp.exp(scores - norm).astype(jnp.bfloat16)
            mixed_head = jnp.dot(probs, head_v, preferred_element_type=jnp.float32).astype(jnp.bfloat16)
            return mixed_head, norm[:, 0]

        mixed_heads, norms_heads = lax.map(one_head, (split_heads(queries), split_heads(keys), split_heads(values)))
        return join_heads(mixed_heads), norms_heads

    mixed, norms = lax.map(forward_group, (query_proj, key_proj, value_proj, rec_starts))
    projected = jnp.dot(mixed.reshape(GROUPS * SEQLEN, D), out_weight, preferred_element_type=jnp.float32)
    projected = projected.astype(jnp.bfloat16).reshape(GROUPS, SEQLEN, D)

    def conv_group(items):
        signal, cot, starts_row = items
        labels = record_ids(frames, starts_row, SEQLEN)
        labels_before = record_ids(before_frames, starts_row, SEQLEN)
        labels_after = record_ids(after_frames, starts_row, SEQLEN)
        padded = jnp.pad(signal, ((LAG, 0), (0, 0)))
        conv = depthwise(padded, labels_before, labels, conv_weight, SEQLEN)
        activated, slope = silu_parts(conv)
        layer = (signal.astype(jnp.float32) + activated).astype(jnp.bfloat16)
        conv_back = cot.astype(jnp.float32) * slope
        back_pad = jnp.pad(conv_back, ((0, LAG), (0, 0)))
        spread = transposed(back_pad, labels_after, labels, conv_weight, SEQLEN)
        proj_back = (cot.astype(jnp.float32) + spread).astype(jnp.bfloat16)
        taps = tap_sums(conv_back, padded, labels_before, labels, KERN)
        return layer, proj_back, taps

    layer_out, proj_back, taps = lax.map(conv_group, (projected, cotangent, rec_starts))
    factor = (GROUPS * SEQLEN) ** -0.5
    conv_grad = jnp.sum(taps, axis=0) * factor

    def group_weight(items):
        return jnp.dot(items[0].T, items[1], preferred_element_type=jnp.float32)

    partials = lax.map(group_weight, (mixed, proj_back))
    weight_grad = jnp.sum(partials, axis=0) * factor
    mixed_back = jnp.dot(proj_back.reshape(GROUPS * SEQLEN, D), out_weight.T, preferred_element_type=jnp.float32)
    mixed_back = mixed_back.astype(jnp.bfloat16).reshape(GROUPS, SEQLEN, D)

    def backward_group(items):
        queries, keys, values, mixed_g, back_g, norms_g, starts_row = items
        labels = record_ids(frames, starts_row, SEQLEN)
        same = labels[:, None] == labels[None, :]

        def one_head(parts):
            head_q, head_k, head_v, head_o, head_d, norm = parts
            scores = head_scores(head_q, head_k, same)
            probs = jnp.exp(scores - norm[:, None]).astype(jnp.bfloat16)
            prob_back = jnp.dot(head_d, head_v.T, preferred_element_type=jnp.float32)
            delta = jnp.sum(head_d.astype(jnp.float32) * head_o.astype(jnp.float32), axis=1)
            score_back = (probs.astype(jnp.float32) * (prob_back - delta[:, None])).astype(jnp.bfloat16)
            grad_q = (scale * jnp.dot(score_back, head_k, preferred_element_type=jnp.float32)).astype(jnp.bfloat16)
            grad_k = (scale * jnp.dot(score_back.T, head_q, preferred_element_type=jnp.float32)).astype(jnp.bfloat16)
            grad_v = jnp.dot(probs.T, head_d, preferred_element_type=jnp.float32).astype(jnp.bfloat16)
            return grad_q, grad_k, grad_v

        grad_q, grad_k, grad_v = lax.map(one_head, (split_heads(queries), split_heads(keys), split_heads(values), split_heads(mixed_g), split_heads(back_g), norms_g))
        return join_heads(grad_q), join_heads(grad_k), join_heads(grad_v)

    query_grad, key_grad, value_grad = lax.map(backward_group, (query_proj, key_proj, value_proj, mixed, mixed_back, norms, rec_starts))
    return layer_out, query_grad, key_grad, value_grad, weight_grad, conv_grad
```

```python
import functools

import jax
import jax.numpy as jnp
from jax import lax
from jax.experimental import pallas as pl
from jax.experimental.pallas import tpu as pltpu
from jax.sharding import PartitionSpec as P

HD = 64
KERN = 31
HALO = 32
BLK = 256
SUB = 3
BIG = 1e30
BF = jnp.bfloat16
F32 = jnp.float32
VM = pl.BlockSpec(memory_space=pltpu.VMEM)
SM = pl.BlockSpec(memory_space=pltpu.SMEM)
ANY = pl.BlockSpec(memory_space=pl.ANY)


def dot(a, b, ca=1, cb=0):
    return lax.dot_general(a, b, (((ca,), (cb,)), ((), ())), preferred_element_type=F32)


def low_lanes(rows):
    return lax.broadcasted_iota(jnp.int32, (rows, 128), 1) < HD


def swap(x):
    return pltpu.roll(x, HD, 1)


def pack_halves(x):
    half = x.shape[0] // 2
    low = low_lanes(half)
    top, bottom = x[:half], x[half:]
    return jnp.where(low, top, swap(bottom)), jnp.where(low, swap(top), bottom)


def unpack_halves(first, second):
    low = low_lanes(first.shape[0])
    return jnp.where(low, first, swap(second)), jnp.where(low, swap(first), second)


def greet(axes):
    barrier = pltpu.get_barrier_semaphore()
    total = 0
    for axis in axes:
        count = lax.axis_size(axis)
        me = lax.axis_index(axis)

        def signal(d, _, axis=axis, count=count, me=me):
            pl.semaphore_signal(barrier, inc=1, device_id={axis: lax.rem(me + d, count)})
            return 0

        lax.fori_loop(1, count, signal, 0)
        total += count - 1
    pl.semaphore_wait(barrier, total)


def rows_at(index, size):
    return pl.ds(pl.multiple_of(index * size, size), size)


def fwd_kernel(
    starts, q_ref, k_ref, v_ref,
    p_out, kf_out, qf_out, kt_out, aux_out, mixed_out,
    kv_send, q_send, kf, q_recv, qf, kt, vt, s_buf, p_buf, aux, mix_send, mix_recv,
    kv_ss, kv_rs, q_ss, q_rs, m_ss, m_rs, p_sem, o_sem,
):
    n = lax.axis_size("seq")
    me = lax.axis_index("seq")
    rows, width = q_ref.shape
    half = rows // 2
    total = n * rows
    chunks = total // BLK
    group = SUB * BLK
    groups = total // group
    owners = group // rows
    for t in range(width // 128):
        cols = pl.ds(t * 128, 128)
        kt_, vt_ = k_ref[:, cols].astype(F32), v_ref[:, cols].astype(F32)
        low = low_lanes(rows)
        kv_send[2 * t] = jnp.where(low, kt_, swap(vt_)).astype(BF)
        kv_send[2 * t + 1] = jnp.where(low, swap(kt_), vt_).astype(BF)
        first, second = pack_halves(q_ref[:, cols].astype(F32) * (HD**-0.5))
        q_send[2 * t] = first.astype(BF)
        q_send[2 * t + 1] = second.astype(BF)
    greet(("seq",))

    def kv_copy(peer, owner, dst_dev):
        return pltpu.make_async_remote_copy(
            src_ref=kv_send.at[peer],
            dst_ref=kf.at[rows_at(owner, rows), pl.ds(0, 128)],
            send_sem=kv_ss.at[peer],
            recv_sem=kv_rs.at[owner],
            device_id={"seq": dst_dev},
        )

    def q_copy(peer, owner, dst_dev):
        return pltpu.make_async_remote_copy(
            src_ref=q_send.at[peer],
            dst_ref=q_recv.at[owner],
            send_sem=q_ss.at[peer],
            recv_sem=q_rs.at[owner],
            device_id={"seq": dst_dev},
        )

    def start(d, _):
        peer = lax.rem(me + d, n)
        kv_copy(peer, me, peer).start()
        q_copy(peer, me, peer).start()
        return 0

    lax.fori_loop(1, n, start, 0)
    kf[rows_at(me, rows), pl.ds(0, 128)] = kv_send[me]
    q_recv[me] = q_send[me]
    second = starts[0, 1]

    def feats(i, _):
        at = lax.broadcasted_iota(jnp.int32, (BLK, 128), 0) + i * BLK
        lane = lax.broadcasted_iota(jnp.int32, (BLK, 128), 1)
        later = jnp.where(at >= second, 1.0, 0.0)
        own = jnp.where(lane == 0, 1.0 - later, jnp.where(lane == 1, later, 0.0))
        other = jnp.where(lane == 0, later, jnp.where(lane == 1, 1.0 - later, 0.0)) * (-BIG)
        ones = jnp.where((lane >= 2) & (lane < 5), 1.0, 0.0)
        kf[rows_at(i, BLK), pl.ds(128, 128)] = (other + ones).astype(BF)
        qf[rows_at(i, BLK), pl.ds(128, 128)] = own.astype(BF)
        return 0

    lax.fori_loop(0, chunks, feats, 0)

    def arrive(d, _):
        src = lax.rem(me - d + n, n)
        kv_copy(me, src, me).wait_recv()
        q_copy(me, src, me).wait_recv()
        return 0

    lax.fori_loop(1, n, arrive, 0)

    def unpack_q(p, _):
        x = q_recv[p].astype(F32)
        low = low_lanes(half)
        qf[rows_at(2 * p, half), pl.ds(0, 128)] = jnp.where(low, x, 0.0).astype(BF)
        qf[rows_at(2 * p + 1, half), pl.ds(0, 128)] = jnp.where(low, swap(x), 0.0).astype(BF)
        return 0

    lax.fori_loop(0, n, unpack_q, 0)
    vt[HD : HD + 16, :] = jnp.ones((16, total), BF)
    for c in range(chunks):
        x = kf[c * BLK : (c + 1) * BLK, 0:128].T
        kt[:, c * BLK : (c + 1) * BLK] = x[:HD]
        vt[0:HD, c * BLK : (c + 1) * BLK] = x[HD:]
    outs = [
        pltpu.make_async_copy(kf, kf_out, o_sem.at[0]),
        pltpu.make_async_copy(qf, qf_out, o_sem.at[1]),
        pltpu.make_async_copy(kt, kt_out, o_sem.at[2]),
    ]
    for copy in outs:
        copy.start()

    def scores(c, q_blk):
        return dot(kf[c * BLK : (c + 1) * BLK, :], q_blk, 1, 1)

    def col_max(best, s):
        return jnp.maximum(best, jnp.max(s.reshape(BLK // 8, 8, BLK), axis=0))

    first_group = me // (n // groups)
    low_start = jnp.full((8, BLK), -3e38, F32)
    q_blk = qf[rows_at(first_group * SUB, BLK), :]
    best = low_start
    for c in range(chunks):
        s = scores(c, q_blk)
        s_buf[0, c * BLK : (c + 1) * BLK, :] = s
        best = col_max(best, s)

    def p_copy(sub, at):
        return pltpu.make_async_copy(p_buf.at[sub], p_out.at[at], p_sem.at[sub])

    def mix_copy(peer, owner, dst_dev):
        return pltpu.make_async_remote_copy(
            src_ref=mix_send.at[peer],
            dst_ref=mix_recv.at[owner],
            send_sem=m_ss.at[peer],
            recv_sem=m_rs.at[owner],
            device_id={"seq": dst_dev},
        )

    def one_group(i, m):
        g = lax.rem(first_group + i, groups)
        g_next = lax.rem(first_group + i + 1, groups)
        for sub in range(SUB):
            at = g * SUB + sub
            ahead = (sub + 1) % SUB
            next_at = at + 1 if sub + 1 < SUB else g_next * SUB

            @pl.when(i > 0)
            def _():
                p_copy(sub, at).wait()

            q_next = qf[rows_at(next_at, BLK), :]
            best = low_start
            acc = jnp.zeros((HD + 16, BLK), F32)
            for c in range(chunks):
                cut = slice(c * BLK, (c + 1) * BLK)
                s = scores(c, q_next)
                s_buf[ahead, cut, :] = s
                best = col_max(best, s)
                p = jnp.exp(s_buf[sub, cut, :] - m).astype(BF)
                p_buf[sub, cut, :] = p
                acc = acc + dot(vt[:, cut], p)
            m = jnp.max(best, axis=0, keepdims=True)
            p_copy(sub, at).start()
            inverse = 1.0 / acc[HD : HD + 1]
            mixed = (acc[:HD] * inverse).astype(BF).astype(F32)
            both = jnp.concatenate([jnp.broadcast_to(inverse, (HD, BLK)), mixed], axis=0)
            aux[rows_at(at, BLK), :] = both.T
        for w in range(owners):
            owner = g * owners + w
            top = aux[rows_at(2 * owner, half), :]
            bottom = aux[rows_at(2 * owner + 1, half), :]
            packed = jnp.where(low_lanes(half), swap(top), bottom).astype(BF)
            mix_send[owner] = packed

            @pl.when(owner != me)
            def _():
                mix_copy(owner, me, owner).start()

            @pl.when(owner == me)
            def _():
                mix_recv[owner] = mix_send[owner]

        return m

    lax.fori_loop(0, groups, one_group, jnp.max(best, axis=0, keepdims=True))
    aux_copy = pltpu.make_async_copy(aux, aux_out, o_sem.at[3])
    aux_copy.start()

    def settle(d, _):
        peer = lax.rem(me + d, n)
        kv_copy(peer, me, peer).wait_send()
        q_copy(peer, me, peer).wait_send()
        mix_copy(peer, me, peer).wait_send()
        mix_copy(me, lax.rem(me - d + n, n), me).wait_recv()
        return 0

    lax.fori_loop(1, n, settle, 0)
    for t in range(width // 128):
        top, bottom = unpack_halves(mix_recv[2 * t].astype(F32), mix_recv[2 * t + 1].astype(F32))
        mixed_out[0:half, t * 128 : (t + 1) * 128] = top.astype(BF)
        mixed_out[half:rows, t * 128 : (t + 1) * 128] = bottom.astype(BF)
    for sub in range(SUB):
        p_copy(sub, 0).wait()
    for copy in outs:
        copy.wait()
    aux_copy.wait()


def forward(starts, q, k, v):
    rows, width = q.shape
    n = lax.axis_size("seq")
    total = n * rows
    half = rows // 2
    shape = jax.ShapeDtypeStruct
    dma = pltpu.SemaphoreType.DMA
    return pl.pallas_call(
        fwd_kernel,
        out_shape=[
            shape((total // BLK, total, BLK), BF),
            shape((total, 256), BF),
            shape((total, 256), BF),
            shape((HD, total), BF),
            shape((total, 128), F32),
            shape((rows, width), BF),
        ],
        in_specs=[SM, VM, VM, VM],
        out_specs=[ANY, ANY, ANY, ANY, ANY, VM],
        scratch_shapes=[
            pltpu.VMEM((n, rows, 128), BF),
            pltpu.VMEM((n, half, 128), BF),
            pltpu.VMEM((total, 256), BF),
            pltpu.VMEM((n, half, 128), BF),
            pltpu.VMEM((total, 256), BF),
            pltpu.VMEM((HD, total), BF),
            pltpu.VMEM((HD + 16, total), BF),
            pltpu.VMEM((SUB, total, BLK), F32),
            pltpu.VMEM((SUB, total, BLK), BF),
            pltpu.VMEM((total, 128), F32),
            pltpu.VMEM((n, half, 128), BF),
            pltpu.VMEM((n, half, 128), BF),
            dma((n,)), dma((n,)), dma((n,)), dma((n,)), dma((n,)), dma((n,)),
            dma((SUB,)), dma((4,)),
        ],
        compiler_params=pltpu.CompilerParams(
            collective_id=0, has_side_effects=True, vmem_limit_bytes=60 * 2**20
        ),
        name="attend",
    )(starts, q, k, v)


def conv_kernel(
    starts, mixed_ref, w_ref, cot_ref, taps_ref,
    layer_out, back_out, wpart_out, cpart_out,
    proj, halo_recv, pad, head, ahead_recv, cpad, pb, back_send, back_recv,
    h_ss, h_rs, a_ss, a_rs, b_ss, b_rs,
):
    n = lax.axis_size("seq")
    me = lax.axis_index("seq")
    rows, width = mixed_ref.shape
    groups = rows // 8
    edge = HALO // 8
    total = n * rows
    second = starts[0, 1]
    base = me * rows
    right, left = lax.rem(me + 1, n), lax.rem(me + n - 1, n)
    step = 256
    for t in range(width // step):
        cut = pl.ds(t * step, step)
        out = dot(mixed_ref[...], w_ref[:, cut]).astype(BF)
        proj[:, cut] = out
        pad[0, HALO : HALO + rows, cut] = out.astype(F32)
    greet(("seq",))
    halo = pltpu.make_async_remote_copy(
        src_ref=proj.at[pl.ds(rows - HALO, HALO)],
        dst_ref=halo_recv,
        send_sem=h_ss,
        recv_sem=h_rs,
        device_id={"seq": right},
    )
    halo.start()

    def frame(first, count):
        return lax.broadcasted_iota(jnp.int32, (count, width), 0) + first

    pad[1, HALO : HALO + rows, :] = jnp.where(
        frame(base, rows) >= second, pad[0, HALO : HALO + rows, :], 0.0
    )

    def later(g):
        return (base + 8 * g >= second).astype(jnp.int32)

    def conv_groups(which):
        def one_tile(t, _):
            cut = rows_at(t, 128)
            w = [jnp.broadcast_to(taps_ref[j : j + 1, cut], (8, 128)) for j in range(KERN)]
            for g in which:
                acc = jnp.zeros((8, 128), F32)
                lab = later(g)
                for j in range(KERN):
                    acc = acc + w[j] * pad[lab, 8 * g + j + 2 : 8 * g + j + 10, cut]
                gate = jax.nn.sigmoid(acc)
                here = slice(8 * g, 8 * g + 8)
                layer = pad[0, HALO + 8 * g : HALO + 8 * g + 8, cut] + acc * gate
                head[here, cut] = layer
                cot = cot_ref[here, cut].astype(F32)
                back = cot * (gate * (1.0 + acc * (1.0 - gate)))
                cpad[1, here, cut] = back
                cpad[0, here, cut] = jnp.where(base + 8 * g < second, back, 0.0)
            return 0

        lax.fori_loop(0, width // 128, one_tile, 0)

    conv_groups(range(edge, groups))
    halo.wait_recv()
    before = halo_recv[...].astype(F32)
    pad[0, 0:HALO, :] = jnp.where(me > 0, before, 0.0)
    pad[1, 0:HALO, :] = jnp.where(
        (frame(base - HALO, HALO) >= second) & (me > 0), before, 0.0
    )
    conv_groups(range(edge))
    pb[0:HALO, :] = cpad[1, 0:HALO, :].astype(BF)
    ahead = pltpu.make_async_remote_copy(
        src_ref=pb.at[pl.ds(0, HALO)],
        dst_ref=ahead_recv,
        send_sem=a_ss,
        recv_sem=a_rs,
        device_id={"seq": left},
    )
    ahead.start()
    layer_out[...] = head[...].astype(BF)

    def spread_groups(which):
        def one_tile(t, _):
            cut = rows_at(t, 128)
            w = [jnp.broadcast_to(taps_ref[j : j + 1, cut], (8, 128)) for j in range(KERN)]
            for g in which:
                acc = cot_ref[8 * g : 8 * g + 8, cut].astype(F32)
                lab = later(g)
                for j in range(KERN):
                    acc = acc + w[j] * cpad[lab, 8 * g + 30 - j : 8 * g + 38 - j, cut]
                head[8 * g : 8 * g + 8, cut] = acc
            return 0

        lax.fori_loop(0, width // 128, one_tile, 0)

    spread_groups(range(groups - edge))
    ahead.wait()
    after = ahead_recv[...].astype(F32)
    inside = me < n - 1
    cpad[1, rows : rows + HALO, :] = jnp.where(inside, after, 0.0)
    cpad[0, rows : rows + HALO, :] = jnp.where(
        (frame(base + rows, HALO) < second) & inside, after, 0.0
    )
    spread_groups(range(groups - edge, groups))
    pb[...] = head[...].astype(BF)
    for t in range(width // step):
        out = dot(pb[...], w_ref[t * step : (t + 1) * step, :], 1, 1).astype(BF).astype(F32)
        for u in range(step // 128):
            first, second_ = pack_halves(out[:, u * 128 : (u + 1) * 128])
            at = 2 * (t * (step // 128) + u)
            back_send[at] = first.astype(BF)
            back_send[at + 1] = second_.astype(BF)

    def back_copy(peer, owner, dst_dev):
        return pltpu.make_async_remote_copy(
            src_ref=back_send.at[peer],
            dst_ref=back_recv.at[owner],
            send_sem=b_ss.at[peer],
            recv_sem=b_rs.at[owner],
            device_id={"seq": dst_dev},
        )

    def start(d, _):
        peer = lax.rem(me + d, n)
        back_copy(peer, me, peer).start()
        return 0

    lax.fori_loop(1, n, start, 0)
    back_recv[me] = back_send[me]
    for t in range(width // step):
        cut = pl.ds(t * step, step)
        wpart_out[cut, :] = dot(mixed_ref[:, cut], pb[...], 0, 0).astype(BF)

    def tap_tile(t, _):
        cut = rows_at(t, 128)
        acc = [jnp.zeros((8, 128), F32)] * KERN
        for g in range(groups):
            lab = later(g)
            signal = cpad[1, 8 * g : 8 * g + 8, cut]
            for j in range(KERN):
                acc[j] = acc[j] + signal * pad[lab, 8 * g + j + 2 : 8 * g + j + 10, cut]
        for j in range(KERN):
            cpart_out[j : j + 1, cut] = jnp.sum(acc[j], axis=0, keepdims=True)
        cpart_out[KERN:, cut] = jnp.zeros((1, 128), F32)
        return 0

    lax.fori_loop(0, width // 128, tap_tile, 0)
    halo.wait_send()

    def settle(d, _):
        peer = lax.rem(me + d, n)
        back_copy(peer, me, peer).wait_send()
        back_copy(me, lax.rem(me - d + n, n), me).wait_recv()
        return 0

    lax.fori_loop(1, n, settle, 0)
    back_out[...] = back_recv[...]


def convolve(starts, mixed, weight, cot, taps):
    rows, width = mixed.shape
    n = lax.axis_size("seq")
    half = rows // 2
    shape = jax.ShapeDtypeStruct
    dma = pltpu.SemaphoreType.DMA
    return pl.pallas_call(
        conv_kernel,
        out_shape=[
            shape((rows, width), BF),
            shape((n, half, 128), BF),
            shape((width, width), BF),
            shape((KERN + 1, width), F32),
        ],
        in_specs=[SM, VM, VM, VM, VM],
        out_specs=[VM, VM, VM, VM],
        scratch_shapes=[
            pltpu.VMEM((rows, width), BF),
            pltpu.VMEM((HALO, width), BF),
            pltpu.VMEM((2, rows + HALO, width), F32),
            pltpu.VMEM((rows, width), F32),
            pltpu.VMEM((HALO, width), BF),
            pltpu.VMEM((2, rows + HALO, width), F32),
            pltpu.VMEM((rows, width), BF),
            pltpu.VMEM((n, half, 128), BF),
            pltpu.VMEM((n, half, 128), BF),
            dma, dma, dma, dma, dma((n,)), dma((n,)),
        ],
        compiler_params=pltpu.CompilerParams(
            collective_id=1, has_side_effects=True, vmem_limit_bytes=60 * 2**20
        ),
        name="convolve",
    )(starts, mixed, weight, cot, taps)


def bwd_kernel(
    p_hbm, kf_ref, qf_ref, kt_ref, aux_ref, back_ref,
    dq_out, dk_out, dv_out,
    of, qd, p_buf, dp, acc_k, acc_v, dqt, kv_send, kv_recv, q_send, q_recv,
    p_sem, kv_ss, kv_rs, q_ss, q_rs,
):
    n = lax.axis_size("seq")
    me = lax.axis_index("seq")
    rows, width = dq_out.shape
    half = rows // 2
    total = n * rows
    chunks = total // BLK
    group = SUB * BLK
    groups = total // group
    owners = group // rows
    first_group = me // (n // groups)

    def p_copy(i):
        g = lax.rem(first_group + i, groups)
        slot = lax.rem(i, 2)
        return pltpu.make_async_copy(
            p_hbm.at[:, rows_at(g, group), :], p_buf.at[slot], p_sem.at[slot]
        )

    p_copy(0).start()

    def prepare(p, _):
        x = back_ref[p].astype(F32)
        low = low_lanes(half)
        lane = lax.broadcasted_iota(jnp.int32, (half, 128), 1)
        for side in range(2):
            at = rows_at(2 * p + side, half)
            side_aux = aux_ref[at, :]
            inverse = jnp.where(low, side_aux, swap(side_aux))
            back = swap(x) if side == 0 else x
            back = jnp.where(low, 0.0, back * inverse).astype(BF)
            wide = back.astype(F32)
            delta = -jnp.sum(wide * side_aux, axis=1, keepdims=True)
            top = delta.astype(BF).astype(F32)
            mid = (delta - top).astype(BF).astype(F32)
            rest = delta - top - mid
            feat = jnp.where(
                lane == 2, top, jnp.where(lane == 3, mid, jnp.where(lane == 4, rest, 0.0))
            )
            of[at, 0:128] = back
            of[at, 128:256] = feat.astype(BF)
            qd[at, :] = (wide + qf_ref[at, 0:128].astype(F32)).astype(BF)
        return 0

    lax.fori_loop(0, n, prepare, 0)
    dqt[...] = jnp.zeros_like(dqt)
    greet(("seq",))

    def kv_copy(peer, owner, dst_dev):
        return pltpu.make_async_remote_copy(
            src_ref=kv_send.at[peer],
            dst_ref=kv_recv.at[owner],
            send_sem=kv_ss.at[peer],
            recv_sem=kv_rs.at[owner],
            device_id={"seq": dst_dev},
        )

    def q_copy(peer, owner, dst_dev):
        return pltpu.make_async_remote_copy(
            src_ref=q_send.at[peer],
            dst_ref=q_recv.at[owner],
            send_sem=q_ss.at[peer],
            recv_sem=q_rs.at[owner],
            device_id={"seq": dst_dev},
        )

    def one_group(i, _):
        g = lax.rem(first_group + i, groups)
        slot = lax.rem(i, 2)

        @pl.when(i + 1 < groups)
        def _():
            p_copy(i + 1).start()

        acc_k[...] = jnp.zeros_like(acc_k)
        acc_v[...] = jnp.zeros_like(acc_v)

        def prob_back(r, c):
            return dot(kf_ref[rows_at(g * SUB + r, BLK), :], of[rows_at(c, BLK), :], 1, 1)

        for r in range(SUB):
            dp[0, r * BLK : (r + 1) * BLK, :] = prob_back(r, 0)
        p_copy(i).wait()

        def two_chunks(pair, _):
            for par in range(2):
                c = 2 * pair + par
                ahead = lax.rem(c + 1, chunks)
                q_d = qd[rows_at(c, BLK), :]
                dq = jnp.zeros((HD, BLK), F32)
                for r in range(SUB):
                    cut = slice(r * BLK, (r + 1) * BLK)
                    dp[1 - par, cut, :] = prob_back(r, ahead)
                    p = p_buf[slot, c, cut, :]
                    ds = (p.astype(F32) * dp[par, cut, :]).astype(BF)
                    acc_v[cut, :] += dot(p, q_d)
                    acc_k[cut, :] += dot(ds, q_d)
                    dq = dq + dot(kt_ref[:, rows_at(g * SUB + r, BLK)], ds)
                dqt[:, rows_at(c, BLK)] += dq
            return 0

        lax.fori_loop(0, chunks // 2, two_chunks, 0)
        for w in range(owners):
            owner = g * owners + w
            cut = slice(w * rows, (w + 1) * rows)
            kv_send[owner] = jnp.where(low_lanes(rows), acc_k[cut, :], acc_v[cut, :]).astype(BF)

            @pl.when(owner != me)
            def _():
                kv_copy(owner, me, owner).start()

            @pl.when(owner == me)
            def _():
                kv_recv[owner] = kv_send[owner]

        return 0

    lax.fori_loop(0, groups, one_group, 0)
    aux = aux_ref
    for c in range(chunks):
        x = dqt[:, c * BLK : (c + 1) * BLK] * (HD**-0.5)
        acc_q = jnp.concatenate([x, jnp.zeros_like(x)], axis=0).T
        aux[c * BLK : (c + 1) * BLK, :] = acc_q

    def send_q(d, _):
        owner = lax.rem(me + d, n)
        top = aux[rows_at(2 * owner, half), :]
        bottom = aux[rows_at(2 * owner + 1, half), :]
        q_send[owner] = jnp.where(low_lanes(half), top, swap(bottom)).astype(BF)

        @pl.when(owner != me)
        def _():
            q_copy(owner, me, owner).start()

        @pl.when(owner == me)
        def _():
            q_recv[owner] = q_send[owner]

        return 0

    lax.fori_loop(1, n + 1, send_q, 0)

    def settle_kv(d, _):
        peer = lax.rem(me + d, n)
        kv_copy(peer, me, peer).wait_send()
        kv_copy(me, lax.rem(me - d + n, n), me).wait_recv()
        return 0

    lax.fori_loop(1, n, settle_kv, 0)
    low = low_lanes(rows)
    for t in range(width // 128):
        cut = slice(t * 128, (t + 1) * 128)
        one, two = kv_recv[2 * t].astype(F32), kv_recv[2 * t + 1].astype(F32)
        dk_out[:, cut] = jnp.where(low, one, swap(two)).astype(BF)
        dv_out[:, cut] = jnp.where(low, swap(one), two).astype(BF)

    def settle_q(d, _):
        peer = lax.rem(me + d, n)
        q_copy(peer, me, peer).wait_send()
        q_copy(me, lax.rem(me - d + n, n), me).wait_recv()
        return 0

    lax.fori_loop(1, n, settle_q, 0)
    for t in range(width // 128):
        cut = slice(t * 128, (t + 1) * 128)
        top, bottom = unpack_halves(q_recv[2 * t].astype(F32), q_recv[2 * t + 1].astype(F32))
        dq_out[0:half, cut] = top.astype(BF)
        dq_out[half:rows, cut] = bottom.astype(BF)


def backward(p, kf, qf, kt, aux, back, rows, width):
    n = lax.axis_size("seq")
    total = n * rows
    half = rows // 2
    shape = jax.ShapeDtypeStruct
    dma = pltpu.SemaphoreType.DMA

    def body(p_hbm, kf_ref, qf_ref, kt_ref, aux_in, back_ref, dq_out, dk_out, dv_out, aux, *rest):
        aux[...] = aux_in[...]
        bwd_kernel(p_hbm, kf_ref, qf_ref, kt_ref, aux, back_ref, dq_out, dk_out, dv_out, *rest)

    return pl.pallas_call(
        body,
        out_shape=[shape((rows, width), BF)] * 3,
        in_specs=[ANY, VM, VM, VM, VM, VM],
        out_specs=[VM, VM, VM],
        scratch_shapes=[
            pltpu.VMEM((total, 128), F32),
            pltpu.VMEM((total, 256), BF),
            pltpu.VMEM((total, 128), BF),
            pltpu.VMEM((2, total // BLK, SUB * BLK, BLK), BF),
            pltpu.VMEM((2, SUB * BLK, BLK), F32),
            pltpu.VMEM((SUB * BLK, 128), F32),
            pltpu.VMEM((SUB * BLK, 128), F32),
            pltpu.VMEM((HD, total), F32),
            pltpu.VMEM((n, rows, 128), BF),
            pltpu.VMEM((n, rows, 128), BF),
            pltpu.VMEM((n, half, 128), BF),
            pltpu.VMEM((n, half, 128), BF),
            dma((2,)), dma((n,)), dma((n,)), dma((n,)), dma((n,)),
        ],
        compiler_params=pltpu.CompilerParams(
            collective_id=2, has_side_effects=True, vmem_limit_bytes=60 * 2**20
        ),
        name="attend_back",
    )(p, kf, qf, kt, aux, back)


def reduce_kernel(
    factor, w_ref, out_ref, one, sums, two, mine, three, part, four, five,
    s1, r1, s2, r2, s3, r3, s4, r4, s5, r5, s6, r6,
):
    n, groups = lax.axis_size("seq"), lax.axis_size("dp")
    me, dp = lax.axis_index("seq"), lax.axis_index("dp")
    width = w_ref.shape[0]
    core, z = lax.rem(me, 2), me // 2
    deep = n // 2
    half = width // 2
    blk = half // groups
    lanes = width // deep
    sibling = me + 1 - 2 * core
    greet(("seq", "dp"))
    c1 = pltpu.make_async_remote_copy(
        src_ref=w_ref.at[rows_at(1 - core, half), :],
        dst_ref=one,
        send_sem=s1,
        recv_sem=r1,
        device_id={"seq": sibling},
    )
    c1.start()
    c1.wait_recv()

    def add(i, _):
        cut = rows_at(i, blk)
        own = w_ref[pl.ds(pl.multiple_of(core * half + i * blk, blk), blk), :]
        sums[cut, :] = (own.astype(F32) + one[cut, :].astype(F32)).astype(BF)
        return 0

    lax.fori_loop(0, groups, add, 0)

    def c2(peer, owner, dev):
        return pltpu.make_async_remote_copy(
            src_ref=sums.at[rows_at(peer, blk), :],
            dst_ref=two.at[owner],
            send_sem=s2.at[peer],
            recv_sem=r2.at[owner],
            device_id={"dp": dev},
        )

    def start2(d, _):
        peer = lax.rem(dp + d, groups)
        c2(peer, dp, peer).start()
        return 0

    lax.fori_loop(1, groups, start2, 0)

    def take2(d, total):
        src = lax.rem(dp - d + groups, groups)
        c2(dp, src, dp).wait_recv()
        return total + two[src].astype(F32)

    total = lax.fori_loop(1, groups, take2, sums[rows_at(dp, blk), :].astype(F32))
    mine[...] = total.astype(BF)

    def at_z(index):
        return index * 2 + core

    def c3(peer, owner, dev):
        return pltpu.make_async_remote_copy(
            src_ref=mine.at[:, rows_at(peer, lanes)],
            dst_ref=three.at[owner],
            send_sem=s3.at[peer],
            recv_sem=r3.at[owner],
            device_id={"seq": at_z(dev)},
        )

    def start3(d, _):
        peer = lax.rem(z + d, deep)
        c3(peer, z, peer).start()
        return 0

    lax.fori_loop(1, deep, start3, 0)

    def take3(d, total):
        src = lax.rem(z - d + deep, deep)
        c3(z, src, z).wait_recv()
        return total + three[src].astype(F32)

    total = lax.fori_loop(1, deep, take3, mine[:, rows_at(z, lanes)].astype(F32))
    part[...] = total.astype(BF)
    four[:, rows_at(z, lanes)] = part[...]

    def c4(peer, owner, dev):
        return pltpu.make_async_remote_copy(
            src_ref=part,
            dst_ref=four.at[:, rows_at(owner, lanes)],
            send_sem=s4.at[peer],
            recv_sem=r4.at[owner],
            device_id={"seq": at_z(dev)},
        )

    def start4(d, _):
        peer = lax.rem(z + d, deep)
        c4(peer, z, peer).start()
        return 0

    lax.fori_loop(1, deep, start4, 0)

    def take4(d, _):
        c4(z, lax.rem(z - d + deep, deep), z).wait_recv()
        return 0

    lax.fori_loop(1, deep, take4, 0)
    five[rows_at(core * groups + dp, blk), :] = four[...]

    def c5(peer, owner, dev):
        return pltpu.make_async_remote_copy(
            src_ref=four,
            dst_ref=five.at[rows_at(core * groups + owner, blk), :],
            send_sem=s5.at[peer],
            recv_sem=r5.at[owner],
            device_id={"dp": dev},
        )

    def start5(d, _):
        peer = lax.rem(dp + d, groups)
        c5(peer, dp, peer).start()
        return 0

    lax.fori_loop(1, groups, start5, 0)

    def take5(d, _):
        c5(dp, lax.rem(dp - d + groups, groups), dp).wait_recv()
        return 0

    lax.fori_loop(1, groups, take5, 0)

    def c6(owner):
        return pltpu.make_async_remote_copy(
            src_ref=five.at[rows_at(owner, half), :],
            dst_ref=five.at[rows_at(owner, half), :],
            send_sem=s6,
            recv_sem=r6,
            device_id={"seq": sibling},
        )

    c6(core).start()
    c6(1 - core).wait_recv()
    for i in range(width // BLK):
        cut = pl.ds(i * BLK, BLK)
        out_ref[cut, :] = five[cut, :].astype(F32) * factor
    c1.wait_send()
    c6(core).wait_send()

    def settle_dp(d, _):
        peer = lax.rem(dp + d, groups)
        c2(peer, dp, peer).wait_send()
        c5(peer, dp, peer).wait_send()
        return 0

    lax.fori_loop(1, groups, settle_dp, 0)

    def settle_z(d, _):
        peer = lax.rem(z + d, deep)
        c3(peer, z, peer).wait_send()
        c4(peer, z, peer).wait_send()
        return 0

    lax.fori_loop(1, deep, settle_z, 0)


def reduce_weight(part, factor):
    width = part.shape[0]
    n, groups = lax.axis_size("seq"), lax.axis_size("dp")
    half, deep = width // 2, n // 2
    blk, lanes = half // groups, width // deep
    dma = pltpu.SemaphoreType.DMA
    return pl.pallas_call(
        functools.partial(reduce_kernel, factor),
        out_shape=jax.ShapeDtypeStruct((width, width), F32),
        in_specs=[VM],
        out_specs=VM,
        scratch_shapes=[
            pltpu.VMEM((half, width), BF),
            pltpu.VMEM((half, width), BF),
            pltpu.VMEM((groups, blk, width), BF),
            pltpu.VMEM((blk, width), BF),
            pltpu.VMEM((deep, blk, lanes), BF),
            pltpu.VMEM((blk, lanes), BF),
            pltpu.VMEM((blk, width), BF),
            pltpu.VMEM((width, width), BF),
            dma, dma, dma((groups,)), dma((groups,)), dma((deep,)), dma((deep,)),
            dma((deep,)), dma((deep,)), dma((groups,)), dma((groups,)), dma, dma,
        ],
        compiler_params=pltpu.CompilerParams(
            collective_id=3, has_side_effects=True, vmem_limit_bytes=40 * 2**20
        ),
        name="reduce_weight",
    )(part)


def local(query_proj, key_proj, value_proj, cotangent, out_weight, conv_weight, rec_starts):
    rows, width = query_proj.shape[1:]
    factor = (lax.axis_size("dp") * lax.axis_size("seq") * rows) ** -0.5
    p, kf, qf, kt, aux, mixed = forward(rec_starts, query_proj[0], key_proj[0], value_proj[0])
    layer, back, weight_part, conv_part = convolve(
        rec_starts, mixed, out_weight, cotangent[0], conv_weight
    )
    conv_grad = lax.psum(conv_part[:KERN], ("dp", "seq")) * factor
    weight_grad = reduce_weight(weight_part, factor)
    dq, dk, dv = backward(p, kf, qf, kt, aux, back, rows, width)
    return layer[None], dq[None], dk[None], dv[None], weight_grad, conv_grad


def solution(mesh):
    frames = P("dp", "seq", None)
    return jax.shard_map(
        local,
        mesh=mesh,
        in_specs=(frames, frames, frames, frames, P(), P(), P("dp", None)),
        out_specs=(frames, frames, frames, frames, P(), P()),
        check_vma=False,
    )
```

```python
import functools

import jax
import jax.numpy as jnp
from jax import lax
from jax.experimental import pallas as pl
from jax.experimental.pallas import tpu as pltpu
from jax.sharding import PartitionSpec as P

HD = 64
KERN = 31
HALO = 32
BLK = 256
SUB = 3
BIG = 1e30
BF = jnp.bfloat16
F32 = jnp.float32
VM = pl.BlockSpec(memory_space=pltpu.VMEM)
SM = pl.BlockSpec(memory_space=pltpu.SMEM)
ANY = pl.BlockSpec(memory_space=pl.ANY)


def dot(a, b, ca=1, cb=0):
    return lax.dot_general(a, b, (((ca,), (cb,)), ((), ())), preferred_element_type=F32)


def low_lanes(rows):
    return lax.broadcasted_iota(jnp.int32, (rows, 128), 1) < HD


def swap(x):
    return pltpu.roll(x, HD, 1)


def pack_halves(x):
    half = x.shape[0] // 2
    low = low_lanes(half)
    top, bottom = x[:half], x[half:]
    return jnp.where(low, top, swap(bottom)), jnp.where(low, swap(top), bottom)


def unpack_halves(first, second):
    low = low_lanes(first.shape[0])
    return jnp.where(low, first, swap(second)), jnp.where(low, swap(first), second)


def greet(axes):
    barrier = pltpu.get_barrier_semaphore()
    total = 0
    for axis in axes:
        count = lax.axis_size(axis)
        me = lax.axis_index(axis)

        def signal(d, _, axis=axis, count=count, me=me):
            pl.semaphore_signal(barrier, inc=1, device_id={axis: lax.rem(me + d, count)})
            return 0

        lax.fori_loop(1, count, signal, 0)
        total += count - 1
    pl.semaphore_wait(barrier, total)


def rows_at(index, size):
    return pl.ds(pl.multiple_of(index * size, size), size)


def fwd_kernel(
    starts, q_ref, k_ref, v_ref,
    p_out, kf_out, qf_out, kt_out, aux_out, mixed_out,
    kv_send, q_send, kf, q_recv, qf, kt, vt, s_buf, p_buf, aux, mix_send, mix_recv,
    kv_ss, kv_rs, q_ss, q_rs, m_ss, m_rs, p_sem, o_sem,
):
    n = lax.axis_size("seq")
    me = lax.axis_index("seq")
    rows, width = q_ref.shape
    half = rows // 2
    total = n * rows
    chunks = total // BLK
    group = SUB * BLK
    groups = total // group
    owners = group // rows
    for t in range(width // 128):
        cols = pl.ds(t * 128, 128)
        kt_, vt_ = k_ref[:, cols].astype(F32), v_ref[:, cols].astype(F32)
        low = low_lanes(rows)
        kv_send[2 * t] = jnp.where(low, kt_, swap(vt_)).astype(BF)
        kv_send[2 * t + 1] = jnp.where(low, swap(kt_), vt_).astype(BF)
        first, second = pack_halves(q_ref[:, cols].astype(F32) * (HD**-0.5))
        q_send[2 * t] = first.astype(BF)
        q_send[2 * t + 1] = second.astype(BF)
    greet(("seq",))

    def kv_copy(peer, owner, dst_dev):
        return pltpu.make_async_remote_copy(
            src_ref=kv_send.at[peer],
            dst_ref=kf.at[rows_at(owner, rows), pl.ds(0, 128)],
            send_sem=kv_ss.at[peer],
            recv_sem=kv_rs.at[owner],
            device_id={"seq": dst_dev},
        )

    def q_copy(peer, owner, dst_dev):
        return pltpu.make_async_remote_copy(
            src_ref=q_send.at[peer],
            dst_ref=q_recv.at[owner],
            send_sem=q_ss.at[peer],
            recv_sem=q_rs.at[owner],
            device_id={"seq": dst_dev},
        )

    def start(d, _):
        peer = lax.rem(me + d, n)
        kv_copy(peer, me, peer).start()
        q_copy(peer, me, peer).start()
        return 0

    lax.fori_loop(1, n, start, 0)
    kf[rows_at(me, rows), pl.ds(0, 128)] = kv_send[me]
    q_recv[me] = q_send[me]
    second = starts[0, 1]

    def feats(i, _):
        at = lax.broadcasted_iota(jnp.int32, (BLK, 128), 0) + i * BLK
        lane = lax.broadcasted_iota(jnp.int32, (BLK, 128), 1)
        later = jnp.where(at >= second, 1.0, 0.0)
        own = jnp.where(lane == 0, 1.0 - later, jnp.where(lane == 1, later, 0.0))
        other = jnp.where(lane == 0, later, jnp.where(lane == 1, 1.0 - later, 0.0)) * (-BIG)
        ones = jnp.where((lane >= 2) & (lane < 5), 1.0, 0.0)
        kf[rows_at(i, BLK), pl.ds(128, 128)] = (other + ones).astype(BF)
        qf[rows_at(i, BLK), pl.ds(128, 128)] = own.astype(BF)
        return 0

    lax.fori_loop(0, chunks, feats, 0)

    def arrive(d, _):
        src = lax.rem(me - d + n, n)
        kv_copy(me, src, me).wait_recv()
        q_copy(me, src, me).wait_recv()
        return 0

    lax.fori_loop(1, n, arrive, 0)

    def unpack_q(p, _):
        x = q_recv[p].astype(F32)
        low = low_lanes(half)
        qf[rows_at(2 * p, half), pl.ds(0, 128)] = jnp.where(low, x, 0.0).astype(BF)
        qf[rows_at(2 * p + 1, half), pl.ds(0, 128)] = jnp.where(low, swap(x), 0.0).astype(BF)
        return 0

    lax.fori_loop(0, n, unpack_q, 0)
    vt[HD : HD + 16, :] = jnp.ones((16, total), BF)
    for c in range(chunks):
        x = kf[c * BLK : (c + 1) * BLK, 0:128].T
        kt[:, c * BLK : (c + 1) * BLK] = x[:HD]
        vt[0:HD, c * BLK : (c + 1) * BLK] = x[HD:]
    outs = [
        pltpu.make_async_copy(kf, kf_out, o_sem.at[0]),
        pltpu.make_async_copy(qf, qf_out, o_sem.at[1]),
        pltpu.make_async_copy(kt, kt_out, o_sem.at[2]),
    ]
    for copy in outs:
        copy.start()

    def scores(c, q_blk):
        return dot(kf[c * BLK : (c + 1) * BLK, :], q_blk, 1, 1)

    def col_max(best, s):
        return jnp.maximum(best, jnp.max(s.reshape(BLK // 8, 8, BLK), axis=0))

    first_group = me // (n // groups)
    low_start = jnp.full((8, BLK), -3e38, F32)
    q_blk = qf[rows_at(first_group * SUB, BLK), :]
    best = low_start
    for c in range(chunks):
        s = scores(c, q_blk)
        s_buf[0, c * BLK : (c + 1) * BLK, :] = s
        best = col_max(best, s)

    def p_copy(sub, at):
        return pltpu.make_async_copy(p_buf.at[sub], p_out.at[at], p_sem.at[sub])

    def mix_copy(peer, owner, dst_dev):
        return pltpu.make_async_remote_copy(
            src_ref=mix_send.at[peer],
            dst_ref=mix_recv.at[owner],
            send_sem=m_ss.at[peer],
            recv_sem=m_rs.at[owner],
            device_id={"seq": dst_dev},
        )

    def one_group(i, m):
        g = lax.rem(first_group + i, groups)
        g_next = lax.rem(first_group + i + 1, groups)
        for sub in range(SUB):
            at = g * SUB + sub
            ahead = (sub + 1) % SUB
            next_at = at + 1 if sub + 1 < SUB else g_next * SUB

            @pl.when(i > 0)
            def _():
                p_copy(sub, at).wait()

            q_next = qf[rows_at(next_at, BLK), :]
            best = low_start
            acc = jnp.zeros((HD + 16, BLK), F32)
            for c in range(chunks):
                cut = slice(c * BLK, (c + 1) * BLK)
                s = scores(c, q_next)
                s_buf[ahead, cut, :] = s
                best = col_max(best, s)
                p = jnp.exp(s_buf[sub, cut, :] - m).astype(BF)
                p_buf[sub, cut, :] = p
                acc = acc + dot(vt[:, cut], p)
            m = jnp.max(best, axis=0, keepdims=True)
            p_copy(sub, at).start()
            inverse = 1.0 / acc[HD : HD + 1]
            mixed = (acc[:HD] * inverse).astype(BF).astype(F32)
            both = jnp.concatenate([jnp.broadcast_to(inverse, (HD, BLK)), mixed], axis=0)
            aux[rows_at(at, BLK), :] = both.T
        for w in range(owners):
            owner = g * owners + w
            top = aux[rows_at(2 * owner, half), :]
            bottom = aux[rows_at(2 * owner + 1, half), :]
            packed = jnp.where(low_lanes(half), swap(top), bottom).astype(BF)
            mix_send[owner] = packed

            @pl.when(owner != me)
            def _():
                mix_copy(owner, me, owner).start()

            @pl.when(owner == me)
            def _():
                mix_recv[owner] = mix_send[owner]

        return m

    lax.fori_loop(0, groups, one_group, jnp.max(best, axis=0, keepdims=True))
    aux_copy = pltpu.make_async_copy(aux, aux_out, o_sem.at[3])
    aux_copy.start()

    def settle(d, _):
        peer = lax.rem(me + d, n)
        kv_copy(peer, me, peer).wait_send()
        q_copy(peer, me, peer).wait_send()
        mix_copy(peer, me, peer).wait_send()
        mix_copy(me, lax.rem(me - d + n, n), me).wait_recv()
        return 0

    lax.fori_loop(1, n, settle, 0)
    for t in range(width // 128):
        top, bottom = unpack_halves(mix_recv[2 * t].astype(F32), mix_recv[2 * t + 1].astype(F32))
        mixed_out[0:half, t * 128 : (t + 1) * 128] = top.astype(BF)
        mixed_out[half:rows, t * 128 : (t + 1) * 128] = bottom.astype(BF)
    for sub in range(SUB):
        p_copy(sub, 0).wait()
    for copy in outs:
        copy.wait()
    aux_copy.wait()


def forward(starts, q, k, v):
    rows, width = q.shape
    n = lax.axis_size("seq")
    total = n * rows
    half = rows // 2
    shape = jax.ShapeDtypeStruct
    dma = pltpu.SemaphoreType.DMA
    return pl.pallas_call(
        fwd_kernel,
        out_shape=[
            shape((total // BLK, total, BLK), BF),
            shape((total, 256), BF),
            shape((total, 256), BF),
            shape((HD, total), BF),
            shape((total, 128), F32),
            shape((rows, width), BF),
        ],
        in_specs=[SM, VM, VM, VM],
        out_specs=[ANY, ANY, ANY, ANY, ANY, VM],
        scratch_shapes=[
            pltpu.VMEM((n, rows, 128), BF),
            pltpu.VMEM((n, half, 128), BF),
            pltpu.VMEM((total, 256), BF),
            pltpu.VMEM((n, half, 128), BF),
            pltpu.VMEM((total, 256), BF),
            pltpu.VMEM((HD, total), BF),
            pltpu.VMEM((HD + 16, total), BF),
            pltpu.VMEM((SUB, total, BLK), F32),
            pltpu.VMEM((SUB, total, BLK), BF),
            pltpu.VMEM((total, 128), F32),
            pltpu.VMEM((n, half, 128), BF),
            pltpu.VMEM((n, half, 128), BF),
            dma((n,)), dma((n,)), dma((n,)), dma((n,)), dma((n,)), dma((n,)),
            dma((SUB,)), dma((4,)),
        ],
        compiler_params=pltpu.CompilerParams(
            collective_id=0, has_side_effects=True, vmem_limit_bytes=60 * 2**20
        ),
        name="attend",
    )(starts, q, k, v)


def conv_kernel(
    starts, mixed_ref, w_ref, cot_ref, taps_ref,
    layer_out, back_out, wpart_out, cpart_out,
    proj, halo_recv, pad, head, ahead_recv, cpad, pb, back_send, back_recv,
    h_ss, h_rs, a_ss, a_rs, b_ss, b_rs,
):
    n = lax.axis_size("seq")
    me = lax.axis_index("seq")
    rows, width = mixed_ref.shape
    groups = rows // 8
    edge = HALO // 8
    total = n * rows
    second = starts[0, 1]
    base = me * rows
    right, left = lax.rem(me + 1, n), lax.rem(me + n - 1, n)
    step = 256
    for t in range(width // step):
        cut = pl.ds(t * step, step)
        out = dot(mixed_ref[...], w_ref[:, cut]).astype(BF)
        proj[:, cut] = out
        pad[0, HALO : HALO + rows, cut] = out.astype(F32)
    greet(("seq",))
    halo = pltpu.make_async_remote_copy(
        src_ref=proj.at[pl.ds(rows - HALO, HALO)],
        dst_ref=halo_recv,
        send_sem=h_ss,
        recv_sem=h_rs,
        device_id={"seq": right},
    )
    halo.start()

    def frame(first, count):
        return lax.broadcasted_iota(jnp.int32, (count, width), 0) + first

    pad[1, HALO : HALO + rows, :] = jnp.where(
        frame(base, rows) >= second, pad[0, HALO : HALO + rows, :], 0.0
    )

    def later(g):
        return (base + 8 * g >= second).astype(jnp.int32)

    def conv_groups(which):
        def one_tile(t, _):
            cut = rows_at(t, 128)
            w = [jnp.broadcast_to(taps_ref[j : j + 1, cut], (8, 128)) for j in range(KERN)]
            for g in which:
                acc = jnp.zeros((8, 128), F32)
                lab = later(g)
                for j in range(KERN):
                    acc = acc + w[j] * pad[lab, 8 * g + j + 2 : 8 * g + j + 10, cut]
                gate = jax.nn.sigmoid(acc)
                here = slice(8 * g, 8 * g + 8)
                layer = pad[0, HALO + 8 * g : HALO + 8 * g + 8, cut] + acc * gate
                head[here, cut] = layer
                cot = cot_ref[here, cut].astype(F32)
                back = cot * (gate * (1.0 + acc * (1.0 - gate)))
                cpad[1, here, cut] = back
                cpad[0, here, cut] = jnp.where(base + 8 * g < second, back, 0.0)
            return 0

        lax.fori_loop(0, width // 128, one_tile, 0)

    conv_groups(range(edge, groups))
    halo.wait_recv()
    before = halo_recv[...].astype(F32)
    pad[0, 0:HALO, :] = jnp.where(me > 0, before, 0.0)
    pad[1, 0:HALO, :] = jnp.where(
        (frame(base - HALO, HALO) >= second) & (me > 0), before, 0.0
    )
    conv_groups(range(edge))
    pb[0:HALO, :] = cpad[1, 0:HALO, :].astype(BF)
    ahead = pltpu.make_async_remote_copy(
        src_ref=pb.at[pl.ds(0, HALO)],
        dst_ref=ahead_recv,
        send_sem=a_ss,
        recv_sem=a_rs,
        device_id={"seq": left},
    )
    ahead.start()
    layer_out[...] = head[...].astype(BF)

    def spread_groups(which):
        def one_tile(t, _):
            cut = rows_at(t, 128)
            w = [jnp.broadcast_to(taps_ref[j : j + 1, cut], (8, 128)) for j in range(KERN)]
            for g in which:
                acc = cot_ref[8 * g : 8 * g + 8, cut].astype(F32)
                lab = later(g)
                for j in range(KERN):
                    acc = acc + w[j] * cpad[lab, 8 * g + 30 - j : 8 * g + 38 - j, cut]
                head[8 * g : 8 * g + 8, cut] = acc
            return 0

        lax.fori_loop(0, width // 128, one_tile, 0)

    spread_groups(range(groups - edge))
    ahead.wait()
    after = ahead_recv[...].astype(F32)
    inside = me < n - 1
    cpad[1, rows : rows + HALO, :] = jnp.where(inside, after, 0.0)
    cpad[0, rows : rows + HALO, :] = jnp.where(
        (frame(base + rows, HALO) < second) & inside, after, 0.0
    )
    spread_groups(range(groups - edge, groups))
    pb[...] = head[...].astype(BF)
    for t in range(width // step):
        out = dot(pb[...], w_ref[t * step : (t + 1) * step, :], 1, 1).astype(BF).astype(F32)
        for u in range(step // 128):
            first, second_ = pack_halves(out[:, u * 128 : (u + 1) * 128])
            at = 2 * (t * (step // 128) + u)
            back_send[at] = first.astype(BF)
            back_send[at + 1] = second_.astype(BF)

    def back_copy(peer, owner, dst_dev):
        return pltpu.make_async_remote_copy(
            src_ref=back_send.at[peer],
            dst_ref=back_recv.at[owner],
            send_sem=b_ss.at[peer],
            recv_sem=b_rs.at[owner],
            device_id={"seq": dst_dev},
        )

    def start(d, _):
        peer = lax.rem(me + d, n)
        back_copy(peer, me, peer).start()
        return 0

    lax.fori_loop(1, n, start, 0)
    back_recv[me] = back_send[me]
    for t in range(width // step):
        cut = pl.ds(t * step, step)
        wpart_out[cut, :] = dot(mixed_ref[:, cut], pb[...], 0, 0).astype(BF)

    def tap_tile(t, _):
        cut = rows_at(t, 128)
        acc = [jnp.zeros((8, 128), F32)] * KERN
        for g in range(groups):
            lab = later(g)
            signal = cpad[1, 8 * g : 8 * g + 8, cut]
            for j in range(KERN):
                acc[j] = acc[j] + signal * pad[lab, 8 * g + j + 2 : 8 * g + j + 10, cut]
        for j in range(KERN):
            cpart_out[j : j + 1, cut] = jnp.sum(acc[j], axis=0, keepdims=True)
        cpart_out[KERN:, cut] = jnp.zeros((1, 128), F32)
        return 0

    lax.fori_loop(0, width // 128, tap_tile, 0)
    halo.wait_send()

    def settle(d, _):
        peer = lax.rem(me + d, n)
        back_copy(peer, me, peer).wait_send()
        back_copy(me, lax.rem(me - d + n, n), me).wait_recv()
        return 0

    lax.fori_loop(1, n, settle, 0)
    back_out[...] = back_recv[...]


def convolve(starts, mixed, weight, cot, taps):
    rows, width = mixed.shape
    n = lax.axis_size("seq")
    half = rows // 2
    shape = jax.ShapeDtypeStruct
    dma = pltpu.SemaphoreType.DMA
    return pl.pallas_call(
        conv_kernel,
        out_shape=[
            shape((rows, width), BF),
            shape((n, half, 128), BF),
            shape((width, width), BF),
            shape((KERN + 1, width), F32),
        ],
        in_specs=[SM, VM, VM, VM, VM],
        out_specs=[VM, VM, VM, VM],
        scratch_shapes=[
            pltpu.VMEM((rows, width), BF),
            pltpu.VMEM((HALO, width), BF),
            pltpu.VMEM((2, rows + HALO, width), F32),
            pltpu.VMEM((rows, width), F32),
            pltpu.VMEM((HALO, width), BF),
            pltpu.VMEM((2, rows + HALO, width), F32),
            pltpu.VMEM((rows, width), BF),
            pltpu.VMEM((n, half, 128), BF),
            pltpu.VMEM((n, half, 128), BF),
            dma, dma, dma, dma, dma((n,)), dma((n,)),
        ],
        compiler_params=pltpu.CompilerParams(
            collective_id=1, has_side_effects=True, vmem_limit_bytes=60 * 2**20
        ),
        name="convolve",
    )(starts, mixed, weight, cot, taps)


def bwd_kernel(
    p_hbm, kf_ref, qf_ref, kt_ref, aux_ref, back_ref, w_ref, conv_ref,
    dq_out, dk_out, dv_out, w_out, conv_out,
    of, qd, p_buf, dp, acc_k, acc_v, dqt, kv_send, kv_recv, q_send, q_recv,
    p_sem, kv_ss, kv_rs, q_ss, q_rs, *reduce_refs,
):
    n = lax.axis_size("seq")
    me = lax.axis_index("seq")
    rows, width = dq_out.shape
    steps = reducer(w_ref, conv_ref, w_out, conv_out, reduce_refs[:12], reduce_refs[12:])
    half = rows // 2
    total = n * rows
    chunks = total // BLK
    group = SUB * BLK
    groups = total // group
    owners = group // rows
    first_group = me // (n // groups)

    def p_copy(i):
        g = lax.rem(first_group + i, groups)
        slot = lax.rem(i, 2)
        return pltpu.make_async_copy(
            p_hbm.at[:, rows_at(g, group), :], p_buf.at[slot], p_sem.at[slot]
        )

    p_copy(0).start()

    def prepare(p, _):
        x = back_ref[p].astype(F32)
        low = low_lanes(half)
        lane = lax.broadcasted_iota(jnp.int32, (half, 128), 1)
        for side in range(2):
            at = rows_at(2 * p + side, half)
            side_aux = aux_ref[at, :]
            inverse = jnp.where(low, side_aux, swap(side_aux))
            back = swap(x) if side == 0 else x
            back = jnp.where(low, 0.0, back * inverse).astype(BF)
            wide = back.astype(F32)
            delta = -jnp.sum(wide * side_aux, axis=1, keepdims=True)
            top = delta.astype(BF).astype(F32)
            mid = (delta - top).astype(BF).astype(F32)
            rest = delta - top - mid
            feat = jnp.where(
                lane == 2, top, jnp.where(lane == 3, mid, jnp.where(lane == 4, rest, 0.0))
            )
            of[at, 0:128] = back
            of[at, 128:256] = feat.astype(BF)
            qd[at, :] = (wide + qf_ref[at, 0:128].astype(F32)).astype(BF)
        return 0

    lax.fori_loop(0, n, prepare, 0)
    dqt[...] = jnp.zeros_like(dqt)
    greet(("seq", "dp"))
    steps[0]()
    places = {0: 1, 2: 2, 3: 3, 4: 4, 6: 5} if groups >= 4 else {0: 1, 1: 2, 2: 3, 3: 4}

    def kv_copy(peer, owner, dst_dev):
        return pltpu.make_async_remote_copy(
            src_ref=kv_send.at[peer],
            dst_ref=kv_recv.at[owner],
            send_sem=kv_ss.at[peer],
            recv_sem=kv_rs.at[owner],
            device_id={"seq": dst_dev},
        )

    def q_copy(peer, owner, dst_dev):
        return pltpu.make_async_remote_copy(
            src_ref=q_send.at[peer],
            dst_ref=q_recv.at[owner],
            send_sem=q_ss.at[peer],
            recv_sem=q_rs.at[owner],
            device_id={"seq": dst_dev},
        )

    def one_group(i, _):
        g = lax.rem(first_group + i, groups)
        slot = lax.rem(i, 2)

        @pl.when(i + 1 < groups)
        def _():
            p_copy(i + 1).start()

        acc_k[...] = jnp.zeros_like(acc_k)
        acc_v[...] = jnp.zeros_like(acc_v)

        def prob_back(r, c):
            return dot(kf_ref[rows_at(g * SUB + r, BLK), :], of[rows_at(c, BLK), :], 1, 1)

        for r in range(SUB):
            dp[0, r * BLK : (r + 1) * BLK, :] = prob_back(r, 0)
        p_copy(i).wait()

        def two_chunks(pair, _):
            for par in range(2):
                c = 2 * pair + par
                ahead = lax.rem(c + 1, chunks)
                q_d = qd[rows_at(c, BLK), :]
                dq = jnp.zeros((HD, BLK), F32)
                for r in range(SUB):
                    cut = slice(r * BLK, (r + 1) * BLK)
                    dp[1 - par, cut, :] = prob_back(r, ahead)
                    p = p_buf[slot, c, cut, :]
                    ds = (p.astype(F32) * dp[par, cut, :]).astype(BF)
                    acc_v[cut, :] += dot(p, q_d)
                    acc_k[cut, :] += dot(ds, q_d)
                    dq = dq + dot(kt_ref[:, rows_at(g * SUB + r, BLK)], ds)
                dqt[:, rows_at(c, BLK)] += dq
            return 0

        for h in range(2):
            lax.fori_loop(h * chunks // 4, (h + 1) * chunks // 4, two_chunks, 0)
            for place, number in places.items():
                if place % 2 == h:
                    pl.when(i == place // 2)(steps[number])
        for w in range(owners):
            owner = g * owners + w
            cut = slice(w * rows, (w + 1) * rows)
            kv_send[owner] = jnp.where(low_lanes(rows), acc_k[cut, :], acc_v[cut, :]).astype(BF)

            @pl.when(owner != me)
            def _():
                kv_copy(owner, me, owner).start()

            @pl.when(owner == me)
            def _():
                kv_recv[owner] = kv_send[owner]

        return 0

    lax.fori_loop(0, groups, one_group, 0)
    aux = aux_ref
    for c in range(chunks):
        x = dqt[:, c * BLK : (c + 1) * BLK] * (HD**-0.5)
        acc_q = jnp.concatenate([x, jnp.zeros_like(x)], axis=0).T
        aux[c * BLK : (c + 1) * BLK, :] = acc_q

    def send_q(d, _):
        owner = lax.rem(me + d, n)
        top = aux[rows_at(2 * owner, half), :]
        bottom = aux[rows_at(2 * owner + 1, half), :]
        q_send[owner] = jnp.where(low_lanes(half), top, swap(bottom)).astype(BF)

        @pl.when(owner != me)
        def _():
            q_copy(owner, me, owner).start()

        @pl.when(owner == me)
        def _():
            q_recv[owner] = q_send[owner]

        return 0

    lax.fori_loop(1, n + 1, send_q, 0)
    if 5 not in places.values():
        steps[5]()

    def settle_kv(d, _):
        peer = lax.rem(me + d, n)
        kv_copy(peer, me, peer).wait_send()
        kv_copy(me, lax.rem(me - d + n, n), me).wait_recv()
        return 0

    lax.fori_loop(1, n, settle_kv, 0)
    steps[6]()
    low = low_lanes(rows)
    for t in range(width // 128):
        cut = slice(t * 128, (t + 1) * 128)
        one, two = kv_recv[2 * t].astype(F32), kv_recv[2 * t + 1].astype(F32)
        dk_out[:, cut] = jnp.where(low, one, swap(two)).astype(BF)
        dv_out[:, cut] = jnp.where(low, swap(one), two).astype(BF)

    def settle_q(d, _):
        peer = lax.rem(me + d, n)
        q_copy(peer, me, peer).wait_send()
        q_copy(me, lax.rem(me - d + n, n), me).wait_recv()
        return 0

    lax.fori_loop(1, n, settle_q, 0)
    for t in range(width // 128):
        cut = slice(t * 128, (t + 1) * 128)
        top, bottom = unpack_halves(q_recv[2 * t].astype(F32), q_recv[2 * t + 1].astype(F32))
        dq_out[0:half, cut] = top.astype(BF)
        dq_out[half:rows, cut] = bottom.astype(BF)


def backward(p, kf, qf, kt, aux, back, w_part, conv_part, rows):
    n, groups = lax.axis_size("seq"), lax.axis_size("dp")
    width = w_part.shape[0]
    bufs, sems = reducer_bufs(width, n, groups)
    total = n * rows
    half = rows // 2
    shape = jax.ShapeDtypeStruct
    dma = pltpu.SemaphoreType.DMA

    def body(p_hbm, kf_ref, qf_ref, kt_ref, aux_in, *rest):
        outs = rest[3:8]
        aux = rest[8]
        aux[...] = aux_in[...]
        bwd_kernel(p_hbm, kf_ref, qf_ref, kt_ref, aux, *rest[:3], *outs, *rest[9:])

    return pl.pallas_call(
        body,
        out_shape=[shape((rows, width), BF)] * 3
        + [shape((width, width), BF), shape((KERN + 1, width), F32)],
        in_specs=[ANY] + [VM] * 7,
        out_specs=[VM] * 5,
        scratch_shapes=[
            pltpu.VMEM((total, 128), F32),
            pltpu.VMEM((total, 256), BF),
            pltpu.VMEM((total, 128), BF),
            pltpu.VMEM((2, total // BLK, SUB * BLK, BLK), BF),
            pltpu.VMEM((2, SUB * BLK, BLK), F32),
            pltpu.VMEM((SUB * BLK, 128), F32),
            pltpu.VMEM((SUB * BLK, 128), F32),
            pltpu.VMEM((HD, total), F32),
            pltpu.VMEM((n, rows, 128), BF),
            pltpu.VMEM((n, rows, 128), BF),
            pltpu.VMEM((n, half, 128), BF),
            pltpu.VMEM((n, half, 128), BF),
            dma((2,)), dma((n,)), dma((n,)), dma((n,)), dma((n,)),
            *bufs, *sems,
        ],
        compiler_params=pltpu.CompilerParams(
            collective_id=2, has_side_effects=True, vmem_limit_bytes=60 * 2**20
        ),
        name="attend_back",
    )(p, kf, qf, kt, aux, back, w_part, conv_part)


def reducer(w_ref, conv_ref, w_out, conv_out, bufs, sems):
    one, sums, two, mine, three, part, four, conv_one, conv_sums, conv_two, conv_three, conv_part = bufs
    s1, r1, s2, r2, s3, r3, s4, r4, s5, r5, s6, r6 = sems
    n, groups = lax.axis_size("seq"), lax.axis_size("dp")
    me, dp = lax.axis_index("seq"), lax.axis_index("dp")
    width = w_ref.shape[0]
    core, z = lax.rem(me, 2), me // 2
    deep = n // 2
    half = width // 2
    blk = half // groups
    lanes = width // deep
    conv_half = (KERN + 1) // 2
    per_row = groups // 2
    conv_lanes = width // per_row
    sibling = me + 1 - 2 * core

    def send(src, dst, ss, rs, dev):
        return pltpu.make_async_remote_copy(
            src_ref=src, dst_ref=dst, send_sem=ss, recv_sem=rs, device_id=dev
        )

    def tile(ref, index, first=0):
        row = pl.multiple_of(first + 8 * (index // per_row), 8)
        return ref.at[pl.ds(row, 8), rows_at(lax.rem(index, per_row), conv_lanes)]

    def c1():
        dev = {"seq": sibling}
        return (
            send(w_ref.at[rows_at(1 - core, half), :], one, s1.at[0], r1.at[0], dev),
            send(conv_ref.at[rows_at(1 - core, conv_half), :], conv_one, s1.at[1], r1.at[1], dev),
        )

    def c2(peer, owner, dev):
        dev = {"dp": dev}
        return (
            send(sums.at[rows_at(peer, blk), :], two.at[owner], s2.at[0, peer], r2.at[0, owner], dev),
            send(tile(conv_sums, peer), conv_two.at[owner], s2.at[1, peer], r2.at[1, owner], dev),
        )

    def c3(peer, owner, dev):
        dev = {"seq": dev * 2 + core}
        return (
            send(mine.at[:, rows_at(peer, lanes)], three.at[owner], s3.at[0, peer], r3.at[0, owner], dev),
            send(conv_part, conv_three.at[owner], s3.at[1, peer], r3.at[1, owner], dev),
        )

    def c4(peer, owner, dev):
        dev = {"seq": dev * 2 + core}
        return (send(part, four.at[:, rows_at(owner, lanes)], s4.at[peer], r4.at[owner], dev),)

    def c5(peer, owner, dev):
        dev = {"dp": dev}
        to = w_out.at[rows_at(core * groups + owner, blk), :]
        return (
            send(four, to, s5.at[0, peer], r5.at[0, owner], dev),
            send(conv_part, tile(conv_out, owner, core * conv_half), s5.at[1, peer], r5.at[1, owner], dev),
        )

    def c6(owner):
        dev = {"seq": sibling}
        here, there = w_out.at[rows_at(owner, half), :], conv_out.at[rows_at(owner, conv_half), :]
        return send(here, here, s6.at[0], r6.at[0], dev), send(there, there, s6.at[1], r6.at[1], dev)

    def to_all(copies, own, count):
        def go(d, _):
            peer = lax.rem(own + d, count)
            for copy in copies(peer, own, peer):
                copy.start()
            return 0

        lax.fori_loop(1, count, go, 0)

    def from_all(copies, own, count):
        def go(d, _):
            for copy in copies(own, lax.rem(own - d + count, count), own):
                copy.wait_recv()
            return 0

        lax.fori_loop(1, count, go, 0)

    def step0():
        for copy in c1():
            copy.start()

    def step1():
        for copy in c1():
            copy.wait_recv()

        def add(i, _):
            cut = rows_at(i, blk)
            own = w_ref[pl.ds(pl.multiple_of(core * half + i * blk, blk), blk), :]
            sums[cut, :] = (own.astype(F32) + one[cut, :].astype(F32)).astype(BF)
            return 0

        lax.fori_loop(0, groups, add, 0)
        conv_sums[...] = conv_ref[rows_at(core, conv_half), :] + conv_one[...]
        to_all(c2, dp, groups)

    def step2():
        from_all(c2, dp, groups)
        two[dp] = sums[rows_at(dp, blk), :]
        conv_two[dp] = tile(conv_sums, dp)[...]

        def add(i, total):
            return total[0] + two[i].astype(F32), total[1] + conv_two[i]

        zero = jnp.zeros((blk, width), F32), jnp.zeros((8, conv_lanes), F32)
        total = lax.fori_loop(0, groups, add, zero)
        mine[...] = total[0].astype(BF)
        conv_part[...] = total[1]
        to_all(c3, z, deep)

    def step3():
        from_all(c3, z, deep)
        three[z] = mine[:, rows_at(z, lanes)]
        conv_three[z] = conv_part[...]
        total, conv_total = jnp.zeros((blk, lanes), F32), jnp.zeros((8, conv_lanes), F32)
        for i in range(deep):
            total = total + three[i].astype(F32)
            conv_total = conv_total + conv_three[i]
        part[...] = total.astype(BF)
        four[:, rows_at(z, lanes)] = part[...]

        def settle(d, _):
            c3(lax.rem(z + d, deep), z, lax.rem(z + d, deep))[1].wait_send()
            return 0

        lax.fori_loop(1, deep, settle, 0)
        conv_part[...] = conv_total
        to_all(c4, z, deep)

    def step4():
        from_all(c4, z, deep)
        w_out[rows_at(core * groups + dp, blk), :] = four[...]
        tile(conv_out, dp, core * conv_half)[...] = conv_part[...]
        to_all(c5, dp, groups)

    def step5():
        from_all(c5, dp, groups)
        for copy in c6(core):
            copy.start()

    def step6():
        for copy in c6(1 - core):
            copy.wait_recv()
        for copy in (*c1(), *c6(core)):
            copy.wait_send()

        def settle_dp(d, _):
            peer = lax.rem(dp + d, groups)
            for copy in (*c2(peer, dp, peer), *c5(peer, dp, peer)):
                copy.wait_send()
            return 0

        lax.fori_loop(1, groups, settle_dp, 0)

        def settle_z(d, _):
            peer = lax.rem(z + d, deep)
            for copy in (c3(peer, z, peer)[0], *c4(peer, z, peer)):
                copy.wait_send()
            return 0

        lax.fori_loop(1, deep, settle_z, 0)

    return step0, step1, step2, step3, step4, step5, step6


def reducer_bufs(width, n, groups):
    half, deep = width // 2, n // 2
    blk, lanes = half // groups, width // deep
    conv_half, conv_lanes = (KERN + 1) // 2, width // (groups // 2)
    dma = pltpu.SemaphoreType.DMA
    bufs = [
        pltpu.VMEM((half, width), BF),
        pltpu.VMEM((half, width), BF),
        pltpu.VMEM((groups, blk, width), BF),
        pltpu.VMEM((blk, width), BF),
        pltpu.VMEM((deep, blk, lanes), BF),
        pltpu.VMEM((blk, lanes), BF),
        pltpu.VMEM((blk, width), BF),
        pltpu.VMEM((conv_half, width), F32),
        pltpu.VMEM((conv_half, width), F32),
        pltpu.VMEM((groups, 8, conv_lanes), F32),
        pltpu.VMEM((deep, 8, conv_lanes), F32),
        pltpu.VMEM((8, conv_lanes), F32),
    ]
    sems = [dma((2,))] * 2 + [dma((2, groups))] * 2 + [dma((2, deep))] * 2 + [dma((deep,))] * 2
    sems += [dma((2, groups))] * 2 + [dma((2,))] * 2
    return bufs, sems


def local(query_proj, key_proj, value_proj, cotangent, out_weight, conv_weight, rec_starts):
    rows, width = query_proj.shape[1:]
    factor = (lax.axis_size("dp") * lax.axis_size("seq") * rows) ** -0.5
    p, kf, qf, kt, aux, mixed = forward(rec_starts, query_proj[0], key_proj[0], value_proj[0])
    layer, back, weight_part, conv_part = convolve(
        rec_starts, mixed, out_weight, cotangent[0], conv_weight
    )
    dq, dk, dv, weight_sum, conv_sum = backward(
        p, kf, qf, kt, aux, back, weight_part, conv_part, rows
    )
    weight_grad = weight_sum.astype(F32) * factor
    conv_grad = conv_sum[:KERN] * factor
    return layer[None], dq[None], dk[None], dv[None], weight_grad, conv_grad


def solution(mesh):
    frames = P("dp", "seq", None)
    return jax.shard_map(
        local,
        mesh=mesh,
        in_specs=(frames, frames, frames, frames, P(), P(), P("dp", None)),
        out_specs=(frames, frames, frames, frames, P(), P()),
        check_vma=False,
    )
```

```python
import functools

import jax
import jax.numpy as jnp
from jax import lax
from jax.experimental import pallas as pl
from jax.experimental.pallas import tpu as pltpu
from jax.sharding import PartitionSpec as P

HD = 64
KERN = 31
HALO = 32
BLK = 256
SUB = 3
BIG = 1e30
BF = jnp.bfloat16
F32 = jnp.float32
VM = pl.BlockSpec(memory_space=pltpu.VMEM)
SM = pl.BlockSpec(memory_space=pltpu.SMEM)
ANY = pl.BlockSpec(memory_space=pl.ANY)


def dot(a, b, ca=1, cb=0):
    return lax.dot_general(a, b, (((ca,), (cb,)), ((), ())), preferred_element_type=F32)


def low_lanes(rows):
    return lax.broadcasted_iota(jnp.int32, (rows, 128), 1) < HD


def swap(x):
    return pltpu.roll(x, HD, 1)


def pack_halves(x):
    half = x.shape[0] // 2
    low = low_lanes(half)
    top, bottom = x[:half], x[half:]
    return jnp.where(low, top, swap(bottom)), jnp.where(low, swap(top), bottom)


def unpack_halves(first, second):
    low = low_lanes(first.shape[0])
    return jnp.where(low, first, swap(second)), jnp.where(low, swap(first), second)


def greet(axes):
    barrier = pltpu.get_barrier_semaphore()
    total = 0
    for axis in axes:
        count = lax.axis_size(axis)
        me = lax.axis_index(axis)

        def signal(d, _, axis=axis, count=count, me=me):
            pl.semaphore_signal(barrier, inc=1, device_id={axis: lax.rem(me + d, count)})
            return 0

        lax.fori_loop(1, count, signal, 0)
        total += count - 1
    pl.semaphore_wait(barrier, total)


def rows_at(index, size):
    return pl.ds(pl.multiple_of(index * size, size), size)


def attend(
    starts, q_ref, k_ref, v_ref, mixed_out,
    qk_send, v_send, qk_recv, v_recv, kx, qx, vx, kt, vt, s_buf, p_buf, aux, mix_send, mix_recv,
    k_ss, k_rs, v_ss, v_rs, m_ss, m_rs,
):
    n = lax.axis_size("seq")
    me = lax.axis_index("seq")
    rows, width = q_ref.shape
    half = rows // 2
    total = n * rows
    chunks = total // BLK
    group = SUB * BLK
    groups = total // group
    early = groups // 2
    owners = group // rows
    for t in range(width // 128):
        cols = pl.ds(t * 128, 128)
        q_, k_ = q_ref[:, cols].astype(F32) * (HD**-0.5), k_ref[:, cols].astype(F32)
        low = low_lanes(rows)
        qk_send[2 * t] = jnp.where(low, q_, swap(k_)).astype(BF)
        qk_send[2 * t + 1] = jnp.where(low, swap(q_), k_).astype(BF)
        first, second = pack_halves(v_ref[:, cols].astype(F32))
        v_send[2 * t] = first.astype(BF)
        v_send[2 * t + 1] = second.astype(BF)
    greet(("seq", "dp"))

    def qk_copy(peer, owner, dst_dev):
        return pltpu.make_async_remote_copy(
            src_ref=qk_send.at[peer],
            dst_ref=qk_recv.at[owner],
            send_sem=k_ss.at[peer],
            recv_sem=k_rs.at[owner],
            device_id={"seq": dst_dev},
        )

    def v_copy(peer, owner, dst_dev):
        return pltpu.make_async_remote_copy(
            src_ref=v_send.at[peer],
            dst_ref=v_recv.at[owner],
            send_sem=v_ss.at[peer],
            recv_sem=v_rs.at[owner],
            device_id={"seq": dst_dev},
        )

    def start_qk(d, _):
        peer = lax.rem(me + d, n)
        qk_copy(peer, me, peer).start()
        return 0

    def start_v(d, _):
        peer = lax.rem(me + d, n)
        v_copy(peer, me, peer).start()
        return 0

    lax.fori_loop(1, n, start_qk, 0)
    lax.fori_loop(1, n, start_v, 0)
    second = starts[0, 1]

    def take_qk(src):
        at = lax.broadcasted_iota(jnp.int32, (rows, 128), 0) + src * rows
        lane = lax.broadcasted_iota(jnp.int32, (rows, 128), 1) - HD
        later = jnp.where(at >= second, 1.0, 0.0)
        own = jnp.where(lane == 0, 1.0 - later, jnp.where(lane == 1, later, 0.0))
        other = jnp.where(lane == 0, later, jnp.where(lane == 1, 1.0 - later, 0.0)) * (-BIG)
        x = qk_recv[src].astype(F32)
        qx[rows_at(src, rows), :] = jnp.where(lane < 0, x, own).astype(BF)
        kx[rows_at(src, rows), :] = jnp.where(lane < 0, swap(x), other).astype(BF)

    qk_recv[me] = qk_send[me]
    take_qk(me)

    def arrive(d, _):
        src = lax.rem(me - d + n, n)
        qk_copy(me, src, me).wait_recv()
        take_qk(src)
        return 0

    lax.fori_loop(1, n, arrive, 0)
    def scores(c, q_blk):
        return dot(kx[c * BLK : (c + 1) * BLK, :], q_blk, 1, 1)

    def col_max(best, s):
        return jnp.maximum(best, jnp.max(s.reshape(BLK // 8, 8, BLK), axis=0))

    first_group = me // (n // groups)
    low_start = jnp.full((8, BLK), -3e38, F32)
    q_blk = qx[rows_at(first_group * SUB, BLK), :]
    best = low_start
    for c in range(chunks):
        s = scores(c, q_blk)
        s_buf[0, c * BLK : (c + 1) * BLK, :] = s
        best = col_max(best, s)

    def mix_copy(peer, owner, dst_dev):
        return pltpu.make_async_remote_copy(
            src_ref=mix_send.at[peer],
            dst_ref=mix_recv.at[owner],
            send_sem=m_ss.at[peer],
            recv_sem=m_rs.at[owner],
            device_id={"seq": dst_dev},
        )

    def finish_block(at, acc):
        inverse = 1.0 / acc[HD : HD + 1]
        mixed = (acc[:HD] * inverse).astype(BF).astype(F32)
        both = jnp.concatenate([jnp.broadcast_to(inverse, (HD, BLK)), mixed], axis=0)
        aux[rows_at(at, BLK), :] = both.T

    def send_group(g):
        for w in range(owners):
            owner = g * owners + w
            top = aux[rows_at(2 * owner, half), :]
            bottom = aux[rows_at(2 * owner + 1, half), :]
            packed = jnp.where(low_lanes(half), swap(top), bottom).astype(BF)
            mix_send[owner] = packed

            @pl.when(owner != me)
            def _():
                mix_copy(owner, me, owner).start()

            @pl.when(owner == me)
            def _():
                mix_recv[owner] = mix_send[owner]

    def one_group(i, m, with_values):
        g = lax.rem(first_group + i, groups)
        g_next = lax.rem(first_group + i + 1, groups)
        for sub in range(SUB):
            at = g * SUB + sub
            ahead = (sub + 1) % SUB
            next_at = at + 1 if sub + 1 < SUB else g_next * SUB
            q_next = qx[rows_at(next_at, BLK), :]
            best = low_start
            acc = jnp.zeros((HD + 16, BLK), F32)
            for c in range(chunks):
                cut = slice(c * BLK, (c + 1) * BLK)
                s = scores(c, q_next)
                s_buf[ahead, cut, :] = s
                best = col_max(best, s)
                p = jnp.exp(s_buf[sub, cut, :] - m).astype(BF)
                p_buf[at, cut, :] = p
                if with_values:
                    acc = acc + dot(vt[:, cut], p)
            m = jnp.max(best, axis=0, keepdims=True)
            if with_values:
                finish_block(at, acc)
        if with_values:
            send_group(g)
        return m

    m = lax.fori_loop(
        0, early, functools.partial(one_group, with_values=False), jnp.max(best, axis=0, keepdims=True)
    )
    v_recv[me] = v_send[me]

    def take_v(src):
        lane = lax.broadcasted_iota(jnp.int32, (half, 128), 1) - HD
        ones = jnp.where((lane >= 0) & (lane < 3), 1.0, 0.0)
        x = v_recv[src].astype(F32)
        vx[rows_at(2 * src, half), :] = jnp.where(lane < 0, x, ones).astype(BF)
        vx[rows_at(2 * src + 1, half), :] = jnp.where(lane < 0, swap(x), ones).astype(BF)

    take_v(me)

    def arrive_v(d, _):
        src = lax.rem(me - d + n, n)
        v_copy(me, src, me).wait_recv()
        take_v(src)
        return 0

    lax.fori_loop(1, n, arrive_v, 0)
    vt[HD : HD + 16, :] = jnp.ones((16, total), BF)
    for c in range(chunks):
        cut = slice(c * BLK, (c + 1) * BLK)
        vt[0:HD, cut] = vx[cut, :].T[:HD]

    def late_values(i, _):
        g = lax.rem(first_group + i, groups)
        for sub in range(SUB):
            acc = jnp.zeros((HD + 16, BLK), F32)
            for c in range(chunks):
                cut = slice(c * BLK, (c + 1) * BLK)
                acc = acc + dot(vt[:, cut], p_buf[g * SUB + sub, cut, :])
            finish_block(g * SUB + sub, acc)
        send_group(g)
        return 0

    lax.fori_loop(0, early, late_values, 0)
    lax.fori_loop(early, groups, functools.partial(one_group, with_values=True), m)
    for c in range(chunks):
        cut = slice(c * BLK, (c + 1) * BLK)
        kt[:, cut] = kx[cut, :].T[:HD]
    def settle(d, _):
        peer = lax.rem(me + d, n)
        qk_copy(peer, me, peer).wait_send()
        v_copy(peer, me, peer).wait_send()
        mix_copy(peer, me, peer).wait_send()
        mix_copy(me, lax.rem(me - d + n, n), me).wait_recv()
        return 0

    lax.fori_loop(1, n, settle, 0)
    for t in range(width // 128):
        top, bottom = unpack_halves(mix_recv[2 * t].astype(F32), mix_recv[2 * t + 1].astype(F32))
        mixed_out[0:half, t * 128 : (t + 1) * 128] = top.astype(BF)
        mixed_out[half:rows, t * 128 : (t + 1) * 128] = bottom.astype(BF)


def convolve(
    starts, mixed_ref, w_ref, cot_ref, taps_ref, layer_out, sums_out, csums_out, start_reduction,
    wpart, cpart, one, conv_one, proj, halo_recv, pad, head, ahead_recv, cpad, pb, back_send, back_recv,
    h_ss, h_rs, a_ss, a_rs, b_ss, b_rs, c_ss, c_rs,
):
    n = lax.axis_size("seq")
    me = lax.axis_index("seq")
    rows, width = mixed_ref.shape
    groups = rows // 8
    edge = HALO // 8
    total = n * rows
    second = starts[0, 1]
    base = me * rows
    right, left = lax.rem(me + 1, n), lax.rem(me + n - 1, n)
    step = 256
    for t in range(width // step):
        cut = pl.ds(t * step, step)
        out = dot(mixed_ref[...], w_ref[:, cut]).astype(BF)
        proj[:, cut] = out
        pad[0, HALO : HALO + rows, cut] = out.astype(F32)
    halo = pltpu.make_async_remote_copy(
        src_ref=proj.at[pl.ds(rows - HALO, HALO)],
        dst_ref=halo_recv,
        send_sem=h_ss,
        recv_sem=h_rs,
        device_id={"seq": right},
    )
    halo.start()

    def frame(first, count):
        return lax.broadcasted_iota(jnp.int32, (count, width), 0) + first

    pad[1, HALO : HALO + rows, :] = jnp.where(
        frame(base, rows) >= second, pad[0, HALO : HALO + rows, :], 0.0
    )

    def later(g):
        return (base + 8 * g >= second).astype(jnp.int32)

    def conv_groups(which):
        def one_tile(t, _):
            cut = rows_at(t, 128)
            w = [jnp.broadcast_to(taps_ref[j : j + 1, cut], (8, 128)) for j in range(KERN)]
            for g in which:
                acc = jnp.zeros((8, 128), F32)
                lab = later(g)
                for j in range(KERN):
                    acc = acc + w[j] * pad[lab, 8 * g + j + 2 : 8 * g + j + 10, cut]
                gate = jax.nn.sigmoid(acc)
                here = slice(8 * g, 8 * g + 8)
                layer = pad[0, HALO + 8 * g : HALO + 8 * g + 8, cut] + acc * gate
                head[here, cut] = layer
                cot = cot_ref[here, cut].astype(F32)
                back = cot * (gate * (1.0 + acc * (1.0 - gate)))
                cpad[1, here, cut] = back
                cpad[0, here, cut] = jnp.where(base + 8 * g < second, back, 0.0)
            return 0

        lax.fori_loop(0, width // 128, one_tile, 0)

    conv_groups(range(edge, groups))
    halo.wait_recv()
    before = halo_recv[...].astype(F32)
    pad[0, 0:HALO, :] = jnp.where(me > 0, before, 0.0)
    pad[1, 0:HALO, :] = jnp.where(
        (frame(base - HALO, HALO) >= second) & (me > 0), before, 0.0
    )
    conv_groups(range(edge))
    pb[0:HALO, :] = cpad[1, 0:HALO, :].astype(BF)
    ahead = pltpu.make_async_remote_copy(
        src_ref=pb.at[pl.ds(0, HALO)],
        dst_ref=ahead_recv,
        send_sem=a_ss,
        recv_sem=a_rs,
        device_id={"seq": left},
    )
    ahead.start()
    layer_out[...] = head[...].astype(BF)

    def spread_groups(which):
        def one_tile(t, _):
            cut = rows_at(t, 128)
            w = [jnp.broadcast_to(taps_ref[j : j + 1, cut], (8, 128)) for j in range(KERN)]
            for g in which:
                acc = cot_ref[8 * g : 8 * g + 8, cut].astype(F32)
                lab = later(g)
                for j in range(KERN):
                    acc = acc + w[j] * cpad[lab, 8 * g + 30 - j : 8 * g + 38 - j, cut]
                head[8 * g : 8 * g + 8, cut] = acc
            return 0

        lax.fori_loop(0, width // 128, one_tile, 0)

    spread_groups(range(groups - edge))
    ahead.wait()
    after = ahead_recv[...].astype(F32)
    inside = me < n - 1
    cpad[1, rows : rows + HALO, :] = jnp.where(inside, after, 0.0)
    cpad[0, rows : rows + HALO, :] = jnp.where(
        (frame(base + rows, HALO) < second) & inside, after, 0.0
    )
    spread_groups(range(groups - edge, groups))
    pb[...] = head[...].astype(BF)
    for t in range(width // step):
        out = dot(pb[...], w_ref[t * step : (t + 1) * step, :], 1, 1).astype(BF).astype(F32)
        for u in range(step // 128):
            first, second_ = pack_halves(out[:, u * 128 : (u + 1) * 128])
            at = 2 * (t * (step // 128) + u)
            back_send[at] = first.astype(BF)
            back_send[at + 1] = second_.astype(BF)

    def back_copy(peer, owner, dst_dev):
        return pltpu.make_async_remote_copy(
            src_ref=back_send.at[peer],
            dst_ref=back_recv.at[owner],
            send_sem=b_ss.at[peer],
            recv_sem=b_rs.at[owner],
            device_id={"seq": dst_dev},
        )

    def start(d, _):
        peer = lax.rem(me + d, n)
        back_copy(peer, me, peer).start()
        return 0

    lax.fori_loop(1, n, start, 0)
    back_recv[me] = back_send[me]
    for t in range(width // step):
        cut = pl.ds(t * step, step)
        wpart[cut, :] = dot(mixed_ref[:, cut], pb[...], 0, 0).astype(BF)
    core = lax.rem(me, 2)
    sibling = me + 1 - 2 * core
    part, conv_part = width // 2, (KERN + 1) // 2
    pair = pltpu.make_async_remote_copy(
        src_ref=wpart.at[rows_at(1 - core, part), :],
        dst_ref=one,
        send_sem=c_ss.at[0],
        recv_sem=c_rs.at[0],
        device_id={"seq": sibling},
    )
    pair.start()

    def tap_tile(t, _):
        cut = rows_at(t, 128)
        acc = [jnp.zeros((8, 128), F32)] * KERN
        for g in range(groups):
            lab = later(g)
            signal = cpad[1, 8 * g : 8 * g + 8, cut]
            for j in range(KERN):
                acc[j] = acc[j] + signal * pad[lab, 8 * g + j + 2 : 8 * g + j + 10, cut]
        for j in range(KERN):
            cpart[j : j + 1, cut] = jnp.sum(acc[j], axis=0, keepdims=True)
        cpart[KERN:, cut] = jnp.zeros((1, 128), F32)
        return 0

    lax.fori_loop(0, width // 128, tap_tile, 0)
    conv_pair = pltpu.make_async_remote_copy(
        src_ref=cpart.at[rows_at(1 - core, conv_part), :],
        dst_ref=conv_one,
        send_sem=c_ss.at[1],
        recv_sem=c_rs.at[1],
        device_id={"seq": sibling},
    )
    conv_pair.start()
    pair.wait()

    def add(i, _):
        own = wpart[pl.ds(pl.multiple_of(core * part + i * 32, 32), 32), :].astype(F32)
        sums_out[rows_at(i, 32), :] = (own + one[rows_at(i, 32), :].astype(F32)).astype(BF)
        return 0

    lax.fori_loop(0, part // 32, add, 0)
    conv_pair.wait()
    csums_out[...] = cpart[rows_at(core, conv_part), :] + conv_one[...]
    start_reduction()
    halo.wait_send()

    def settle(d, _):
        peer = lax.rem(me + d, n)
        back_copy(peer, me, peer).wait_send()
        back_copy(me, lax.rem(me - d + n, n), me).wait_recv()
        return 0

    lax.fori_loop(1, n, settle, 0)


def attend_back(
    p_buf, vx, qx, kt, aux, back, kv_recv, q_recv, steps,
    of, qd, s_buf, dqt, kv_send, q_send, kv_ss, kv_rs, q_ss, q_rs,
):
    n = lax.axis_size("seq")
    me = lax.axis_index("seq")
    rows = kv_recv.shape[1]
    half = rows // 2
    total = n * rows
    chunks = total // BLK
    group = SUB * BLK
    groups = total // group
    owners = group // rows
    first_group = me // (n // groups)
    first_chunk = first_group * SUB

    def prepare(p, _):
        x = back[p].astype(F32)
        low = low_lanes(half)
        lane = lax.broadcasted_iota(jnp.int32, (half, 128), 1) - HD
        for side in range(2):
            at = rows_at(2 * p + side, half)
            side_aux = aux[at, :]
            got = jnp.where(low, (x if side == 0 else swap(x)) * side_aux, 0.0)
            got = got.astype(BF).astype(F32)
            delta = -jnp.sum(got * swap(side_aux), axis=1, keepdims=True)
            top = delta.astype(BF).astype(F32)
            mid = (delta - top).astype(BF).astype(F32)
            rest = delta - top - mid
            feat = jnp.where(
                lane == 0, top, jnp.where(lane == 1, mid, jnp.where(lane == 2, rest, 0.0))
            )
            of[at, :] = jnp.where(low, got, feat).astype(BF)
            qd[at, :] = jnp.where(low, qx[at, :].astype(F32), swap(got)).astype(BF)
        return 0

    lax.fori_loop(0, n, prepare, 0)
    dqt[...] = jnp.zeros_like(dqt)
    places = {2: 1, 3: 2, 4: 3} if groups >= 4 else {0: 1, 1: 2, 2: 3}
    acc_k, acc_v = s_buf.at[1, 0:group, 0:128], s_buf.at[1, 0:group, 128:256]
    halves = chunks % 4 == 0

    def kv_copy(peer, owner, dst_dev):
        return pltpu.make_async_remote_copy(
            src_ref=kv_send.at[peer],
            dst_ref=kv_recv.at[owner],
            send_sem=kv_ss.at[peer],
            recv_sem=kv_rs.at[owner],
            device_id={"seq": dst_dev},
        )

    def q_copy(peer, owner, dst_dev):
        return pltpu.make_async_remote_copy(
            src_ref=q_send.at[peer],
            dst_ref=q_recv.at[owner],
            send_sem=q_ss.at[peer],
            recv_sem=q_rs.at[owner],
            device_id={"seq": dst_dev},
        )

    def send_q(side):
        def turn(j, _):
            c = lax.rem(first_chunk + j, chunks)
            x = dqt[:, rows_at(c, BLK)] * (HD**-0.5)
            aux[rows_at(c, BLK), :] = jnp.concatenate([x, jnp.zeros_like(x)], axis=0).T
            return 0

        lax.fori_loop(side * chunks // 2, (side + 1) * chunks // 2, turn, 0)

        def send(d, _):
            owner = lax.rem(first_group * owners + d, n)
            top = aux[rows_at(2 * owner, half), :]
            bottom = aux[rows_at(2 * owner + 1, half), :]
            q_send[owner] = jnp.where(low_lanes(half), top, swap(bottom)).astype(BF)

            @pl.when(owner != me)
            def _():
                q_copy(owner, me, owner).start()

            @pl.when(owner == me)
            def _():
                q_recv[owner] = q_send[owner]

            return 0

        lax.fori_loop(side * n // 2, (side + 1) * n // 2, send, 0)

    def one_group(i, _):
        g = lax.rem(first_group + i, groups)
        acc_k[...] = jnp.zeros_like(acc_k)
        acc_v[...] = jnp.zeros_like(acc_v)

        def prob_back(r, c):
            return dot(vx[rows_at(g * SUB + r, BLK), :], of[rows_at(c, BLK), :], 1, 1)

        for r in range(SUB):
            s_buf[0, r * BLK : (r + 1) * BLK, :] = prob_back(r, first_chunk)

        def two_chunks(pair, _):
            for par in range(2):
                c = lax.rem(2 * pair + par + first_chunk, chunks)
                ahead = lax.rem(c + 1, chunks)
                q_d = qd[rows_at(c, BLK), :]
                dq = jnp.zeros((HD, BLK), F32)
                for r in range(SUB):
                    cut = slice(r * BLK, (r + 1) * BLK)
                    keys = rows_at(g * SUB + r, BLK)
                    there = slice((1 - par) * group + r * BLK, (1 - par) * group + (r + 1) * BLK)
                    here = slice(par * group + r * BLK, par * group + (r + 1) * BLK)
                    s_buf[0, there, :] = prob_back(r, ahead)
                    p = p_buf[c, keys, :]
                    ds = (p.astype(F32) * s_buf[0, here, :]).astype(BF)
                    acc_v[cut, :] += dot(p, q_d)
                    acc_k[cut, :] += dot(ds, q_d)
                    dq = dq + dot(kt[:, keys], ds)
                dqt[:, rows_at(c, BLK)] += dq
            return 0

        for h in range(2):
            lax.fori_loop(h * chunks // 4, (h + 1) * chunks // 4, two_chunks, 0)
            for place, number in places.items():
                if place % 2 == h:
                    pl.when(i == place // 2)(steps[number])
            if h == 0 and halves:
                pl.when(i == groups - 1)(functools.partial(send_q, 0))
        for w in range(owners):
            owner = g * owners + w
            cut = slice(w * rows, (w + 1) * rows)
            kv_send[owner] = jnp.where(low_lanes(rows), acc_k[cut, :], acc_v[cut, :]).astype(BF)

            @pl.when(owner != me)
            def _():
                kv_copy(owner, me, owner).start()

            @pl.when(owner == me)
            def _():
                kv_recv[owner] = kv_send[owner]

        return 0

    lax.fori_loop(0, groups, one_group, 0)
    for side in range(1 if halves else 0, 2):
        send_q(side)

    def settle_kv(d, _):
        peer = lax.rem(me + d, n)
        kv_copy(peer, me, peer).wait_send()
        kv_copy(me, lax.rem(me - d + n, n), me).wait_recv()
        return 0

    lax.fori_loop(1, n, settle_kv, 0)
    steps[4]()

    def settle_q(d, _):
        peer = lax.rem(me + d, n)
        q_copy(peer, me, peer).wait_send()
        q_copy(me, lax.rem(me - d + n, n), me).wait_recv()
        return 0

    lax.fori_loop(1, n, settle_q, 0)
    steps[5]()


def layer_kernel(
    starts, q_ref, k_ref, v_ref, w_hbm, cot_hbm, taps_hbm,
    layer_out, kv_recv, q_recv, w_out, conv_out,
    w_ref, cot_ref, taps_ref, mixed, sums, conv_sums,
    kx, qx, vx, kt, s_buf, p_buf, aux, back_recv, in_sem, *rest,
):
    rest = list(rest)

    def take(count):
        taken = rest[:count]
        del rest[:count]
        return taken

    loads = [
        pltpu.make_async_copy(w_hbm, w_ref, in_sem.at[0]),
        pltpu.make_async_copy(cot_hbm, cot_ref, in_sem.at[1]),
        pltpu.make_async_copy(taps_hbm, taps_ref, in_sem.at[2]),
    ]
    for load in loads:
        load.start()
    qk_send, v_send, qk_recv, v_recv, vt, mix_send, mix_recv = take(7)
    attend(
        starts, q_ref, k_ref, v_ref, mixed,
        qk_send, v_send, qk_recv, v_recv, kx, qx, vx, kt, vt, s_buf, p_buf, aux, mix_send, mix_recv,
        *take(6),
    )
    for load in loads:
        load.wait()
    bufs = take(12)
    sems = take(8)
    reduce_bufs = take(8)
    steps = reducer(sums, conv_sums, w_out, conv_out, reduce_bufs, take(10))
    convolve(
        starts, mixed, w_ref, cot_ref, taps_ref, layer_out, sums, conv_sums, steps[0],
        *bufs, back_recv, *sems,
    )
    of, qd, dqt, kv_send, q_send = take(5)
    attend_back(
        p_buf, vx, qx, kt, aux, back_recv, kv_recv, q_recv, steps,
        of, qd, s_buf, dqt, kv_send, q_send, *rest,
    )


def layer(starts, q, k, v, weight, cot, taps):
    rows, width = q.shape
    n, groups = lax.axis_size("seq"), lax.axis_size("dp")
    total, half = n * rows, rows // 2
    shape, vmem, dma = jax.ShapeDtypeStruct, pltpu.VMEM, pltpu.SemaphoreType.DMA
    bufs, sems = reducer_bufs(width, n, groups)
    wide, narrow = vmem((n, rows, 128), BF), vmem((n, half, 128), BF)
    per_peer = dma((n,))
    return pl.pallas_call(
        layer_kernel,
        out_shape=[
            shape((rows, width), BF),
            shape((n, rows, 128), BF),
            shape((n, half, 128), BF),
            shape((width, width), BF),
            shape((KERN + 1, width), F32),
        ],
        in_specs=[SM, VM, VM, VM, ANY, ANY, ANY],
        out_specs=[VM] * 5,
        scratch_shapes=[
            vmem((width, width), BF), vmem((rows, width), BF), vmem((KERN, width), F32),
            vmem((rows, width), BF),
            vmem((width // 2, width), BF), vmem(((KERN + 1) // 2, width), F32),
            vmem((total, 128), BF), vmem((total, 128), BF), vmem((total, 128), BF),
            vmem((HD, total), BF),
            vmem((SUB, total, BLK), F32), vmem((total // BLK, total, BLK), BF),
            vmem((total, 128), F32), narrow, dma((3,)),
            wide, narrow, wide, narrow, vmem((HD + 16, total), BF), narrow, narrow,
            *[per_peer] * 6,
            vmem((width, width), BF), vmem((KERN + 1, width), F32),
            vmem((width // 2, width), BF), vmem(((KERN + 1) // 2, width), F32),
            vmem((rows, width), BF), vmem((HALO, width), BF), vmem((2, rows + HALO, width), F32),
            vmem((rows, width), F32), vmem((HALO, width), BF), vmem((2, rows + HALO, width), F32),
            vmem((rows, width), BF), narrow,
            dma, dma, dma, dma, per_peer, per_peer, dma((2,)), dma((2,)),
            *bufs, *sems,
            vmem((total, 128), BF), vmem((total, 128), BF), vmem((HD, total), F32), wide, narrow,
            *[per_peer] * 4,
        ],
        compiler_params=pltpu.CompilerParams(
            collective_id=0, has_side_effects=True, vmem_limit_bytes=62 * 2**20 - 2**19
        ),
        name="layer",
    )(starts, q, k, v, weight, cot, taps)


def finish_kernel(
    factor, kv_ref, q_ref, layer_ref, w_ref, conv_ref, layer_out, dq_out, dk_out, dv_out, w_out, conv_out
):
    rows = kv_ref.shape[1]
    half = rows // 2
    low = low_lanes(rows)
    one, two = kv_ref[0].astype(F32), kv_ref[1].astype(F32)
    dk_out[...] = jnp.where(low, one, swap(two)).astype(BF)
    dv_out[...] = jnp.where(low, swap(one), two).astype(BF)
    top, bottom = unpack_halves(q_ref[0].astype(F32), q_ref[1].astype(F32))
    dq_out[0:half, :] = top.astype(BF)
    dq_out[half:rows, :] = bottom.astype(BF)
    layer_out[...] = layer_ref[...]
    w_out[...] = w_ref[...].astype(F32) * factor
    conv_out[...] = conv_ref[0:KERN, :] * factor


def finish(kv, q, layer, w_sum, conv_sum, factor):
    rows, width = layer.shape
    steps = width // 128
    shape = jax.ShapeDtypeStruct
    column = pl.BlockSpec((rows, 128), lambda t: (0, t))
    band = pl.BlockSpec((width // steps, width), lambda t: (t, 0))
    return pl.pallas_call(
        functools.partial(finish_kernel, factor),
        grid=(steps,),
        out_shape=[shape((rows, width), BF)] * 4
        + [shape((width, width), F32), shape((KERN, width), F32)],
        in_specs=[
            pl.BlockSpec((2, rows, 128), lambda t: (t, 0, 0)),
            pl.BlockSpec((2, rows // 2, 128), lambda t: (t, 0, 0)),
            column,
            band,
            pl.BlockSpec((KERN + 1, 128), lambda t: (0, t)),
        ],
        out_specs=[column] * 4 + [band, pl.BlockSpec((KERN, 128), lambda t: (0, t))],
        name="finish",
    )(kv, q, layer, w_sum, conv_sum)


def reducer(sums, conv_sums, w_out, conv_out, bufs, sems):
    two, mine, three, part, four, conv_two, conv_three, conv_part = bufs
    s2, r2, s3, r3, s4, r4, s5, r5, s6, r6 = sems
    n, groups = lax.axis_size("seq"), lax.axis_size("dp")
    me, dp = lax.axis_index("seq"), lax.axis_index("dp")
    width = w_out.shape[0]
    core, z = lax.rem(me, 2), me // 2
    deep = n // 2
    half = width // 2
    blk = half // groups
    lanes = width // deep
    conv_half = (KERN + 1) // 2
    per_row = groups // 2
    conv_lanes = width // per_row
    sibling = me + 1 - 2 * core

    def send(src, dst, ss, rs, dev):
        return pltpu.make_async_remote_copy(
            src_ref=src, dst_ref=dst, send_sem=ss, recv_sem=rs, device_id=dev
        )

    def tile(ref, index, first=0):
        row = pl.multiple_of(first + 8 * (index // per_row), 8)
        return ref.at[pl.ds(row, 8), rows_at(lax.rem(index, per_row), conv_lanes)]

    def c2(peer, owner, dev):
        dev = {"dp": dev}
        return (
            send(sums.at[rows_at(peer, blk), :], two.at[owner], s2.at[0, peer], r2.at[0, owner], dev),
            send(tile(conv_sums, peer), conv_two.at[owner], s2.at[1, peer], r2.at[1, owner], dev),
        )

    def c3(peer, owner, dev):
        dev = {"seq": dev * 2 + core}
        return (
            send(mine.at[:, rows_at(peer, lanes)], three.at[owner], s3.at[0, peer], r3.at[0, owner], dev),
            send(conv_part, conv_three.at[owner], s3.at[1, peer], r3.at[1, owner], dev),
        )

    def c4(peer, owner, dev):
        dev = {"seq": dev * 2 + core}
        return (send(part, four.at[:, rows_at(owner, lanes)], s4.at[peer], r4.at[owner], dev),)

    def c5(peer, owner, dev):
        dev = {"dp": dev}
        to = w_out.at[rows_at(core * groups + owner, blk), :]
        return (
            send(four, to, s5.at[0, peer], r5.at[0, owner], dev),
            send(conv_part, tile(conv_out, owner, core * conv_half), s5.at[1, peer], r5.at[1, owner], dev),
        )

    def c6(owner):
        dev = {"seq": sibling}
        here, there = w_out.at[rows_at(owner, half), :], conv_out.at[rows_at(owner, conv_half), :]
        return send(here, here, s6.at[0], r6.at[0], dev), send(there, there, s6.at[1], r6.at[1], dev)

    def to_all(copies, own, count):
        def go(d, _):
            peer = lax.rem(own + d, count)
            for copy in copies(peer, own, peer):
                copy.start()
            return 0

        lax.fori_loop(1, count, go, 0)

    def from_all(copies, own, count):
        def go(d, _):
            for copy in copies(own, lax.rem(own - d + count, count), own):
                copy.wait_recv()
            return 0

        lax.fori_loop(1, count, go, 0)

    def step1():
        to_all(c2, dp, groups)

    def step2():
        from_all(c2, dp, groups)
        two[dp] = sums[rows_at(dp, blk), :]
        conv_two[dp] = tile(conv_sums, dp)[...]

        def add(i, total):
            return total[0] + two[i].astype(F32), total[1] + conv_two[i]

        zero = jnp.zeros((blk, width), F32), jnp.zeros((8, conv_lanes), F32)
        total = lax.fori_loop(0, groups, add, zero)
        mine[...] = total[0].astype(BF)
        conv_part[...] = total[1]
        to_all(c3, z, deep)

    def step3():
        from_all(c3, z, deep)
        three[z] = mine[:, rows_at(z, lanes)]
        conv_three[z] = conv_part[...]
        total, conv_total = jnp.zeros((blk, lanes), F32), jnp.zeros((8, conv_lanes), F32)
        for i in range(deep):
            total = total + three[i].astype(F32)
            conv_total = conv_total + conv_three[i]
        part[...] = total.astype(BF)
        four[:, rows_at(z, lanes)] = part[...]

        def settle(d, _):
            c3(lax.rem(z + d, deep), z, lax.rem(z + d, deep))[1].wait_send()
            return 0

        lax.fori_loop(1, deep, settle, 0)
        conv_part[...] = conv_total
        to_all(c4, z, deep)

    def step4():
        from_all(c4, z, deep)
        w_out[rows_at(core * groups + dp, blk), :] = four[...]
        tile(conv_out, dp, core * conv_half)[...] = conv_part[...]
        to_all(c5, dp, groups)

    def step5():
        from_all(c5, dp, groups)
        for copy in c6(core):
            copy.start()

    def step6():
        for copy in c6(1 - core):
            copy.wait_recv()
        for copy in c6(core):
            copy.wait_send()

        def settle_dp(d, _):
            peer = lax.rem(dp + d, groups)
            for copy in (*c2(peer, dp, peer), *c5(peer, dp, peer)):
                copy.wait_send()
            return 0

        lax.fori_loop(1, groups, settle_dp, 0)

        def settle_z(d, _):
            peer = lax.rem(z + d, deep)
            for copy in (c3(peer, z, peer)[0], *c4(peer, z, peer)):
                copy.wait_send()
            return 0

        lax.fori_loop(1, deep, settle_z, 0)

    return step1, step2, step3, step4, step5, step6


def reducer_bufs(width, n, groups):
    half, deep = width // 2, n // 2
    blk, lanes = half // groups, width // deep
    conv_lanes = width // (groups // 2)
    dma = pltpu.SemaphoreType.DMA
    bufs = [
        pltpu.VMEM((groups, blk, width), BF),
        pltpu.VMEM((blk, width), BF),
        pltpu.VMEM((deep, blk, lanes), BF),
        pltpu.VMEM((blk, lanes), BF),
        pltpu.VMEM((blk, width), BF),
        pltpu.VMEM((groups, 8, conv_lanes), F32),
        pltpu.VMEM((deep, 8, conv_lanes), F32),
        pltpu.VMEM((8, conv_lanes), F32),
    ]
    sems = [dma((2, groups))] * 2 + [dma((2, deep))] * 2 + [dma((deep,))] * 2
    sems += [dma((2, groups))] * 2 + [dma((2,))] * 2
    return bufs, sems


def local(query_proj, key_proj, value_proj, cotangent, out_weight, conv_weight, rec_starts):
    rows, width = query_proj.shape[1:]
    factor = (lax.axis_size("dp") * lax.axis_size("seq") * rows) ** -0.5
    out, kv, q, weight_sum, conv_sum = layer(
        rec_starts, query_proj[0], key_proj[0], value_proj[0], out_weight, cotangent[0], conv_weight
    )
    out, dq, dk, dv, weight_grad, conv_grad = finish(kv, q, out, weight_sum, conv_sum, factor)
    return out[None], dq[None], dk[None], dv[None], weight_grad, conv_grad


def solution(mesh):
    frames = P("dp", "seq", None)
    return jax.shard_map(
        local,
        mesh=mesh,
        in_specs=(frames, frames, frames, frames, P(), P(), P("dp", None)),
        out_specs=(frames, frames, frames, frames, P(), P()),
        check_vma=False,
    )
```

```python
import functools

import jax
import jax.numpy as jnp
from jax import lax
from jax.experimental import pallas as pl
from jax.experimental.pallas import tpu as pltpu
from jax.sharding import PartitionSpec as P

HD = 64
KERN = 31
HALO = 32
BLK = 256
SUB = 3
STEPS = 2
BIG = 1e30
BF = jnp.bfloat16
F32 = jnp.float32
VM = pl.BlockSpec(memory_space=pltpu.VMEM)
SM = pl.BlockSpec(memory_space=pltpu.SMEM)
ANY = pl.BlockSpec(memory_space=pl.ANY)


def dot(a, b, ca=1, cb=0):
    return lax.dot_general(a, b, (((ca,), (cb,)), ((), ())), preferred_element_type=F32)


def low_lanes(rows):
    return lax.broadcasted_iota(jnp.int32, (rows, 128), 1) < HD


def swap(x):
    return pltpu.roll(x, HD, 1)


def pack_halves(x):
    half = x.shape[0] // 2
    low = low_lanes(half)
    top, bottom = x[:half], x[half:]
    return jnp.where(low, top, swap(bottom)), jnp.where(low, swap(top), bottom)


def unpack_halves(first, second):
    low = low_lanes(first.shape[0])
    return jnp.where(low, first, swap(second)), jnp.where(low, swap(first), second)


def greet(axes):
    barrier = pltpu.get_barrier_semaphore()
    total = 0
    for axis in axes:
        count = lax.axis_size(axis)
        me = lax.axis_index(axis)

        def signal(d, _, axis=axis, count=count, me=me):
            pl.semaphore_signal(barrier, inc=1, device_id={axis: lax.rem(me + d, count)})
            return 0

        lax.fori_loop(1, count, signal, 0)
        total += count - 1
    return total


def ring_order(n):
    deep = n // 2
    order = []
    for far in range(deep // 2 - 1, 1, -1):
        order += [(far, 0), (-far, 0), (far, 1), (-far, 1)]
    order += [(deep // 2, 0), (0, 1), (deep // 2, 1), (0, 0)]
    return order + [(1, 0), (-1, 0), (1, 1), (-1, 1)]


def slot_owners(n):
    me = lax.axis_index("seq")
    core, z = lax.rem(me, 2), me // 2
    deep = n // 2
    owners = []
    for steps, other in ring_order(n):
        owner = 2 * lax.rem(z + (steps + deep) % deep, deep) + (1 - core if other else core)
        owners.append((owner, steps == 0 and not other))
    return owners


def rows_at(index, size):
    return pl.ds(pl.multiple_of(index * size, size), size)


def attend(
    starts, q_ref, k_ref, v_ref, loads, greeted, mixed_out,
    qk_send, v_send, qk_recv, v_recv, kx, qx, vx, kt, vt, s_buf, p_buf, aux, mix_send, mix_recv,
    k_ss, k_rs, v_ss, v_rs, m_ss, m_rs,
):
    n = lax.axis_size("seq")
    me = lax.axis_index("seq")
    rows, width = q_ref.shape
    half = rows // 2
    total = n * rows
    chunks = total // BLK
    group = SUB * BLK
    groups = total // group
    early = groups // 2
    owners = group // rows
    slots = slot_owners(n)
    for load in loads[:2]:
        load.wait()
    for t in range(width // 128):
        cols = pl.ds(t * 128, 128)
        q_, k_ = q_ref[:, cols].astype(F32) * (HD**-0.5), k_ref[:, cols].astype(F32)
        low = low_lanes(rows)
        qk_send[2 * t] = jnp.where(low, q_, swap(k_)).astype(BF)
        qk_send[2 * t + 1] = jnp.where(low, swap(q_), k_).astype(BF)
    pl.semaphore_wait(pltpu.get_barrier_semaphore(), greeted)

    def qk_copy(peer, owner, dst_dev):
        return pltpu.make_async_remote_copy(
            src_ref=qk_send.at[peer],
            dst_ref=qk_recv.at[owner],
            send_sem=k_ss.at[peer],
            recv_sem=k_rs.at[owner],
            device_id={"seq": dst_dev},
        )

    def v_copy(peer, owner, dst_dev):
        return pltpu.make_async_remote_copy(
            src_ref=v_send.at[peer],
            dst_ref=v_recv.at[owner],
            send_sem=v_ss.at[peer],
            recv_sem=v_rs.at[owner],
            device_id={"seq": dst_dev},
        )

    for peer, own in slots:
        if not own:
            qk_copy(peer, me, peer).start()
    loads[2].wait()
    for t in range(width // 128):
        first, second = pack_halves(v_ref[:, t * 128 : (t + 1) * 128].astype(F32))
        v_send[2 * t] = first.astype(BF)
        v_send[2 * t + 1] = second.astype(BF)
    for peer, own in slots:
        if not own:
            v_copy(peer, me, peer).start()
    second = starts[0, 1]

    def take_qk(slot, src):
        at = lax.broadcasted_iota(jnp.int32, (rows, 128), 0) + src * rows
        lane = lax.broadcasted_iota(jnp.int32, (rows, 128), 1) - HD
        later = jnp.where(at >= second, 1.0, 0.0)
        own = jnp.where(lane == 0, 1.0 - later, jnp.where(lane == 1, later, 0.0))
        other = jnp.where(lane == 0, later, jnp.where(lane == 1, 1.0 - later, 0.0)) * (-BIG)
        x = qk_recv[src].astype(F32)
        qx[slot * rows : (slot + 1) * rows, :] = jnp.where(lane < 0, x, own).astype(BF)
        kx[slot * rows : (slot + 1) * rows, :] = jnp.where(lane < 0, swap(x), other).astype(BF)

    qk_recv[me] = qk_send[me]
    for slot, (src, own) in enumerate(slots):
        if not own:
            qk_copy(me, src, me).wait_recv()
        take_qk(slot, src)

    def scores(c, q_blk):
        return dot(kx[c * BLK : (c + 1) * BLK, :], q_blk, 1, 1)

    def col_max(best, s):
        return jnp.maximum(best, jnp.max(s.reshape(BLK // 8, 8, BLK), axis=0))

    low_start = jnp.full((8, BLK), -3e38, F32)
    q_blk = qx[0:BLK, :]
    best = low_start
    for c in range(chunks):
        s = scores(c, q_blk)
        s_buf[0, c * BLK : (c + 1) * BLK, :] = s
        best = col_max(best, s)

    def mix_copy(peer, owner, dst_dev):
        return pltpu.make_async_remote_copy(
            src_ref=mix_send.at[peer],
            dst_ref=mix_recv.at[owner],
            send_sem=m_ss.at[peer],
            recv_sem=m_rs.at[owner],
            device_id={"seq": dst_dev},
        )

    def finish_block(at, acc):
        inverse = 1.0 / acc[HD : HD + 1]
        mixed = (acc[:HD] * inverse).astype(BF).astype(F32)
        both = jnp.concatenate([jnp.broadcast_to(inverse, (HD, BLK)), mixed], axis=0)
        aux[rows_at(at, BLK), :] = both.T

    def send_some(g):
        for slot in range(g * owners, (g + 1) * owners):
            owner, own = slots[slot]
            top = aux[slot * rows : slot * rows + half, :]
            bottom = aux[slot * rows + half : (slot + 1) * rows, :]
            mix_send[owner] = jnp.where(low_lanes(half), swap(top), bottom).astype(BF)
            if own:
                mix_recv[owner] = mix_send[owner]
            else:
                mix_copy(owner, me, owner).start()

    def send_group(i):
        for g in range(groups):
            pl.when(i == g)(functools.partial(send_some, g))

    def one_group(i, m, with_values):
        g = i
        g_next = lax.rem(i + 1, groups)
        for sub in range(SUB):
            at = g * SUB + sub
            ahead = (sub + 1) % SUB
            next_at = at + 1 if sub + 1 < SUB else g_next * SUB
            q_next = qx[rows_at(next_at, BLK), :]
            best = low_start
            acc = jnp.zeros((HD + 16, BLK), F32)
            for c in range(chunks):
                cut = slice(c * BLK, (c + 1) * BLK)
                s = scores(c, q_next)
                s_buf[ahead, cut, :] = s
                best = col_max(best, s)
                p = jnp.exp(s_buf[sub, cut, :] - m).astype(BF)
                p_buf[at, cut, :] = p
                if with_values:
                    acc = acc + dot(vt[:, cut], p)
            m = jnp.max(best, axis=0, keepdims=True)
            if with_values:
                finish_block(at, acc)
        if with_values:
            send_group(g)
        return m

    m = lax.fori_loop(
        0, early, functools.partial(one_group, with_values=False), jnp.max(best, axis=0, keepdims=True)
    )
    v_recv[me] = v_send[me]
    lane = lax.broadcasted_iota(jnp.int32, (half, 128), 1) - HD
    ones = jnp.where((lane >= 0) & (lane < 3), 1.0, 0.0)
    for slot, (src, own) in enumerate(slots):
        if not own:
            v_copy(me, src, me).wait_recv()
        x = v_recv[src].astype(F32)
        at = slot * rows
        vx[at : at + half, :] = jnp.where(lane < 0, x, ones).astype(BF)
        vx[at + half : at + rows, :] = jnp.where(lane < 0, swap(x), ones).astype(BF)
    vt[HD : HD + 16, :] = jnp.ones((16, total), BF)
    for c in range(chunks):
        cut = slice(c * BLK, (c + 1) * BLK)
        vt[0:HD, cut] = vx[cut, :].T[:HD]

    def late_values(i, _):
        g = i
        for sub in range(SUB):
            acc = jnp.zeros((HD + 16, BLK), F32)
            for c in range(chunks):
                cut = slice(c * BLK, (c + 1) * BLK)
                acc = acc + dot(vt[:, cut], p_buf[g * SUB + sub, cut, :])
            finish_block(g * SUB + sub, acc)
        send_group(g)
        return 0

    lax.fori_loop(0, early, late_values, 0)
    lax.fori_loop(early, groups, functools.partial(one_group, with_values=True), m)
    for c in range(chunks):
        cut = slice(c * BLK, (c + 1) * BLK)
        kt[:, cut] = kx[cut, :].T[:HD]
    def settle(d, _):
        peer = lax.rem(me + d, n)
        qk_copy(peer, me, peer).wait_send()
        v_copy(peer, me, peer).wait_send()
        mix_copy(peer, me, peer).wait_send()
        mix_copy(me, lax.rem(me - d + n, n), me).wait_recv()
        return 0

    lax.fori_loop(1, n, settle, 0)
    for t in range(width // 128):
        top, bottom = unpack_halves(mix_recv[2 * t].astype(F32), mix_recv[2 * t + 1].astype(F32))
        mixed_out[0:half, t * 128 : (t + 1) * 128] = top.astype(BF)
        mixed_out[half:rows, t * 128 : (t + 1) * 128] = bottom.astype(BF)


def convolve(
    starts, mixed_ref, w_ref, cot_ref, taps_ref, layer_out, sums_out, csums_out, start_reduction,
    wpart, cpart, one, conv_one, proj, halo_recv, pad, head, ahead_recv, cpad, pb, back_send, back_recv,
    h_ss, h_rs, a_ss, a_rs, b_ss, b_rs, c_ss, c_rs,
):
    n = lax.axis_size("seq")
    me = lax.axis_index("seq")
    rows, width = mixed_ref.shape
    groups = rows // 8
    edge = HALO // 8
    total = n * rows
    second = starts[0, 1]
    base = me * rows
    right, left = lax.rem(me + 1, n), lax.rem(me + n - 1, n)
    step = 256
    for t in range(width // step):
        cut = pl.ds(t * step, step)
        out = dot(mixed_ref[...], w_ref[:, cut]).astype(BF)
        proj[:, cut] = out
        pad[0, HALO : HALO + rows, cut] = out.astype(F32)
    halo = pltpu.make_async_remote_copy(
        src_ref=proj.at[pl.ds(rows - HALO, HALO)],
        dst_ref=halo_recv,
        send_sem=h_ss,
        recv_sem=h_rs,
        device_id={"seq": right},
    )
    halo.start()

    def frame(first, count):
        return lax.broadcasted_iota(jnp.int32, (count, width), 0) + first

    pad[1, HALO : HALO + rows, :] = jnp.where(
        frame(base, rows) >= second, pad[0, HALO : HALO + rows, :], 0.0
    )

    def later(g):
        return (base + 8 * g >= second).astype(jnp.int32)

    def conv_groups(which):
        def one_tile(t, _):
            cut = rows_at(t, 128)
            w = [jnp.broadcast_to(taps_ref[j : j + 1, cut], (8, 128)) for j in range(KERN)]
            for g in which:
                acc = jnp.zeros((8, 128), F32)
                lab = later(g)
                for j in range(KERN):
                    acc = acc + w[j] * pad[lab, 8 * g + j + 2 : 8 * g + j + 10, cut]
                gate = jax.nn.sigmoid(acc)
                here = slice(8 * g, 8 * g + 8)
                layer = pad[0, HALO + 8 * g : HALO + 8 * g + 8, cut] + acc * gate
                head[here, cut] = layer
                cot = cot_ref[here, cut].astype(F32)
                back = cot * (gate * (1.0 + acc * (1.0 - gate)))
                cpad[1, here, cut] = back
                cpad[0, here, cut] = jnp.where(base + 8 * g < second, back, 0.0)
            return 0

        lax.fori_loop(0, width // 128, one_tile, 0)

    conv_groups(range(edge, groups))
    halo.wait_recv()
    before = halo_recv[...].astype(F32)
    pad[0, 0:HALO, :] = jnp.where(me > 0, before, 0.0)
    pad[1, 0:HALO, :] = jnp.where(
        (frame(base - HALO, HALO) >= second) & (me > 0), before, 0.0
    )
    conv_groups(range(edge))
    pb[0:HALO, :] = cpad[1, 0:HALO, :].astype(BF)
    ahead = pltpu.make_async_remote_copy(
        src_ref=pb.at[pl.ds(0, HALO)],
        dst_ref=ahead_recv,
        send_sem=a_ss,
        recv_sem=a_rs,
        device_id={"seq": left},
    )
    ahead.start()
    layer_out[...] = head[...].astype(BF)

    def spread_groups(which):
        def one_tile(t, _):
            cut = rows_at(t, 128)
            w = [jnp.broadcast_to(taps_ref[j : j + 1, cut], (8, 128)) for j in range(KERN)]
            for g in which:
                acc = cot_ref[8 * g : 8 * g + 8, cut].astype(F32)
                lab = later(g)
                for j in range(KERN):
                    acc = acc + w[j] * cpad[lab, 8 * g + 30 - j : 8 * g + 38 - j, cut]
                head[8 * g : 8 * g + 8, cut] = acc
            return 0

        lax.fori_loop(0, width // 128, one_tile, 0)

    spread_groups(range(groups - edge))
    ahead.wait()
    after = ahead_recv[...].astype(F32)
    inside = me < n - 1
    cpad[1, rows : rows + HALO, :] = jnp.where(inside, after, 0.0)
    cpad[0, rows : rows + HALO, :] = jnp.where(
        (frame(base + rows, HALO) < second) & inside, after, 0.0
    )
    spread_groups(range(groups - edge, groups))
    pb[...] = head[...].astype(BF)
    for t in range(width // step):
        out = dot(pb[...], w_ref[t * step : (t + 1) * step, :], 1, 1).astype(BF).astype(F32)
        for u in range(step // 128):
            first, second_ = pack_halves(out[:, u * 128 : (u + 1) * 128])
            at = 2 * (t * (step // 128) + u)
            back_send[at] = first.astype(BF)
            back_send[at + 1] = second_.astype(BF)

    def back_copy(peer, owner, dst_dev):
        return pltpu.make_async_remote_copy(
            src_ref=back_send.at[peer],
            dst_ref=back_recv.at[owner],
            send_sem=b_ss.at[peer],
            recv_sem=b_rs.at[owner],
            device_id={"seq": dst_dev},
        )

    for peer, own in slot_owners(n):
        if not own:
            back_copy(peer, me, peer).start()
    back_recv[me] = back_send[me]
    for t in range(width // step):
        cut = pl.ds(t * step, step)
        wpart[cut, :] = dot(mixed_ref[:, cut], pb[...], 0, 0).astype(BF)
    core = lax.rem(me, 2)
    sibling = me + 1 - 2 * core
    part, conv_part = width // 2, (KERN + 1) // 2
    pair = pltpu.make_async_remote_copy(
        src_ref=wpart.at[rows_at(1 - core, part), :],
        dst_ref=one,
        send_sem=c_ss.at[0],
        recv_sem=c_rs.at[0],
        device_id={"seq": sibling},
    )
    pair.start()

    def tap_tile(t, _):
        cut = rows_at(t, 128)
        acc = [jnp.zeros((8, 128), F32)] * KERN
        for g in range(groups):
            lab = later(g)
            signal = cpad[1, 8 * g : 8 * g + 8, cut]
            for j in range(KERN):
                acc[j] = acc[j] + signal * pad[lab, 8 * g + j + 2 : 8 * g + j + 10, cut]
        for j in range(KERN):
            cpart[j : j + 1, cut] = jnp.sum(acc[j], axis=0, keepdims=True)
        cpart[KERN:, cut] = jnp.zeros((1, 128), F32)
        return 0

    lax.fori_loop(0, width // 128, tap_tile, 0)
    conv_pair = pltpu.make_async_remote_copy(
        src_ref=cpart.at[rows_at(1 - core, conv_part), :],
        dst_ref=conv_one,
        send_sem=c_ss.at[1],
        recv_sem=c_rs.at[1],
        device_id={"seq": sibling},
    )
    conv_pair.start()
    pair.wait()

    def add(i, _):
        own = wpart[pl.ds(pl.multiple_of(core * part + i * 32, 32), 32), :].astype(F32)
        sums_out[rows_at(i, 32), :] = (own + one[rows_at(i, 32), :].astype(F32)).astype(BF)
        return 0

    lax.fori_loop(0, part // 32, add, 0)
    conv_pair.wait()
    csums_out[...] = cpart[rows_at(core, conv_part), :] + conv_one[...]
    start_reduction()
    halo.wait_send()

    def arrived(src):
        back_copy(me, src, me).wait_recv()

    def settle(d, _):
        peer = lax.rem(me + d, n)
        back_copy(peer, me, peer).wait_send()
        return 0

    return arrived, lambda: lax.fori_loop(1, n, settle, 0)


def attend_back(
    p_buf, vx, qx, kt, aux, back, arrived, kv_recv, q_recv, copies, steps,
    of, qd, s_buf, dqt, kv_send, q_send, kv_ss, kv_rs, q_ss, q_rs,
):
    n = lax.axis_size("seq")
    me = lax.axis_index("seq")
    rows = kv_recv.shape[1]
    half = rows // 2
    total = n * rows
    chunks = total // BLK
    group = SUB * BLK
    groups = total // group
    owners = group // rows
    slots = slot_owners(n)

    def prepare(slot, src):
        x = back[src].astype(F32)
        low = low_lanes(half)
        lane = lax.broadcasted_iota(jnp.int32, (half, 128), 1) - HD
        for side in range(2):
            at = slice(slot * rows + side * half, slot * rows + (side + 1) * half)
            side_aux = aux[at, :]
            got = jnp.where(low, (x if side == 0 else swap(x)) * side_aux, 0.0)
            got = got.astype(BF).astype(F32)
            delta = -jnp.sum(got * swap(side_aux), axis=1, keepdims=True)
            top = delta.astype(BF).astype(F32)
            mid = (delta - top).astype(BF).astype(F32)
            rest = delta - top - mid
            feat = jnp.where(
                lane == 0, top, jnp.where(lane == 1, mid, jnp.where(lane == 2, rest, 0.0))
            )
            of[at, :] = jnp.where(low, got, feat).astype(BF)
            qd[at, :] = jnp.where(low, qx[at, :].astype(F32), swap(got)).astype(BF)

    dqt[...] = jnp.zeros_like(dqt)
    for slot, (src, own) in enumerate(slots):
        if not own:
            arrived(src)
        prepare(slot, src)
    places = {1: 1, 2: 2, 3: 3, 7: 4} if groups >= 4 else {0: 1, 1: 2, 2: 3, 3: 4}
    acc_k, acc_v = s_buf.at[1, 0:group, 0:128], s_buf.at[1, 0:group, 128:256]
    halves = chunks % 4 == 0

    def kv_copy(peer, owner, dst_dev):
        return pltpu.make_async_remote_copy(
            src_ref=kv_send.at[peer],
            dst_ref=kv_recv.at[owner],
            send_sem=kv_ss.at[peer],
            recv_sem=kv_rs.at[owner],
            device_id={"seq": dst_dev},
        )

    def q_copy(peer, owner, dst_dev):
        return pltpu.make_async_remote_copy(
            src_ref=q_send.at[peer],
            dst_ref=q_recv.at[owner],
            send_sem=q_ss.at[peer],
            recv_sem=q_rs.at[owner],
            device_id={"seq": dst_dev},
        )

    def send_q(side):
        def turn(j, _):
            c = j
            x = dqt[:, rows_at(c, BLK)] * (HD**-0.5)
            aux[rows_at(c, BLK), :] = jnp.concatenate([x, jnp.zeros_like(x)], axis=0).T
            return 0

        lax.fori_loop(side * chunks // 2, (side + 1) * chunks // 2, turn, 0)

        for slot in range(side * n // 2, (side + 1) * n // 2):
            owner, own = slots[slot]
            top = aux[slot * rows : slot * rows + half, :]
            bottom = aux[slot * rows + half : (slot + 1) * rows, :]
            q_send[owner] = jnp.where(low_lanes(half), top, swap(bottom)).astype(BF)
            if own:
                q_recv[owner] = q_send[owner]
            else:
                q_copy(owner, me, owner).start()

    def send_kv(g):
        for w in range(owners):
            owner, own = slots[g * owners + w]
            cut = slice(w * rows, (w + 1) * rows)
            kv_send[owner] = jnp.where(low_lanes(rows), acc_k[cut, :], acc_v[cut, :]).astype(BF)
            if own:
                kv_recv[owner] = kv_send[owner]
            else:
                kv_copy(owner, me, owner).start()

    def hooks(i, h):
        for place, number in places.items():
            if place % 2 == h:
                pl.when(i == place // 2)(steps[number])

    def one_group(i, _):
        g = i
        acc_k[...] = jnp.zeros_like(acc_k)
        acc_v[...] = jnp.zeros_like(acc_v)

        def prob_back(r, c):
            return dot(vx[rows_at(g * SUB + r, BLK), :], of[rows_at(c, BLK), :], 1, 1)

        for r in range(SUB):
            s_buf[0, r * BLK : (r + 1) * BLK, :] = prob_back(r, 0)

        def two_chunks(pair, _):
            for par in range(2):
                c = 2 * pair + par
                ahead = lax.rem(c + 1, chunks)
                q_d = qd[rows_at(c, BLK), :]
                dq = jnp.zeros((HD, BLK), F32)
                for r in range(SUB):
                    cut = slice(r * BLK, (r + 1) * BLK)
                    keys = rows_at(g * SUB + r, BLK)
                    there = slice((1 - par) * group + r * BLK, (1 - par) * group + (r + 1) * BLK)
                    here = slice(par * group + r * BLK, par * group + (r + 1) * BLK)
                    s_buf[0, there, :] = prob_back(r, ahead)
                    p = p_buf[c, keys, :]
                    ds = (p.astype(F32) * s_buf[0, here, :]).astype(BF)
                    acc_v[cut, :] += dot(p, q_d)
                    acc_k[cut, :] += dot(ds, q_d)
                    dq = dq + dot(kt[:, keys], ds)
                dqt[:, rows_at(c, BLK)] += dq
            return 0

        for h in range(2):
            lax.fori_loop(h * chunks // 4, (h + 1) * chunks // 4, two_chunks, 0)
            if h == 0:
                hooks(i, h)
                if halves:
                    pl.when(i == groups - 1)(functools.partial(send_q, 0))
        for group_at in range(groups):
            pl.when(i == group_at)(functools.partial(send_kv, group_at))
        hooks(i, 1)
        return 0

    lax.fori_loop(0, groups, one_group, 0)
    for side in range(1 if halves else 0, 2):
        send_q(side)

    steps[5]()
    copies[0].start()
    copies[1].start()

    def settle_kv(d, _):
        peer = lax.rem(me + d, n)
        kv_copy(peer, me, peer).wait_send()
        kv_copy(me, lax.rem(me - d + n, n), me).wait_recv()
        return 0

    lax.fori_loop(1, n, settle_kv, 0)
    copies[2].start()

    def settle_q(d, _):
        peer = lax.rem(me + d, n)
        q_copy(peer, me, peer).wait_send()
        q_copy(me, lax.rem(me - d + n, n), me).wait_recv()
        return 0

    lax.fori_loop(1, n, settle_q, 0)
    copies[3].start()


def layer_kernel(
    starts, q_hbm, k_hbm, v_hbm, w_hbm, cot_hbm, taps_hbm,
    layer_hbm, kv_hbm, qg_hbm, w_out_hbm, conv_hbm,
    q_ref, k_ref, v_ref, w_ref, cot_ref, taps_ref, layer_out, kv_recv, q_recv, w_out, conv_out,
    mixed, sums, conv_sums, kx, qx, vx, kt, s_buf, p_buf, aux, back_recv, in_sem, out_sem, *rest,
):
    rest = list(rest)

    def take(count):
        taken = rest[:count]
        del rest[:count]
        return taken

    greeted = greet(("seq", "dp"))
    sources = (q_hbm, k_hbm, v_hbm, w_hbm, cot_hbm, taps_hbm)
    places = (q_ref, k_ref, v_ref, w_ref, cot_ref, taps_ref)
    loads = [
        pltpu.make_async_copy(source, place, in_sem.at[i])
        for i, (source, place) in enumerate(zip(sources, places))
    ]
    for load in loads:
        load.start()
    results = ((w_out, w_out_hbm), (conv_out, conv_hbm), (kv_recv, kv_hbm), (q_recv, qg_hbm), (layer_out, layer_hbm))
    copies = [
        pltpu.make_async_copy(source, place, out_sem.at[i]) for i, (source, place) in enumerate(results)
    ]
    qk_send, v_send, qk_recv, v_recv, vt, mix_send, mix_recv = take(7)
    attend(
        starts, q_ref, k_ref, v_ref, loads, greeted, mixed,
        qk_send, v_send, qk_recv, v_recv, kx, qx, vx, kt, vt, s_buf, p_buf, aux, mix_send, mix_recv,
        *take(6),
    )
    for load in loads[3:]:
        load.wait()
    bufs = take(12)
    sems = take(8)
    reduce_bufs = take(8)
    steps = reducer(sums, conv_sums, w_out, conv_out, reduce_bufs, take(10))
    arrived, settle_back = convolve(
        starts, mixed, w_ref, cot_ref, taps_ref, layer_out, sums, conv_sums, steps[0],
        *bufs, back_recv, *sems,
    )
    copies[4].start()
    of, qd, dqt, kv_send, q_send = take(5)
    attend_back(
        p_buf, vx, qx, kt, aux, back_recv, arrived, kv_recv, q_recv, copies, steps,
        of, qd, s_buf, dqt, kv_send, q_send, *rest,
    )
    settle_back()
    for copy in copies:
        copy.wait()


def layer(starts, q, k, v, weight, cot, taps):
    rows, width = q.shape
    n, groups = lax.axis_size("seq"), lax.axis_size("dp")
    total, half = n * rows, rows // 2
    shape, vmem, dma = jax.ShapeDtypeStruct, pltpu.VMEM, pltpu.SemaphoreType.DMA
    bufs, sems = reducer_bufs(width, n, groups)
    wide, narrow, square = vmem((n, rows, 128), BF), vmem((n, half, 128), BF), vmem((width, width), BF)
    frames, lanes = vmem((rows, width), BF), vmem((total, 128), BF)
    taps_all, taps_half = vmem((KERN + 1, width), F32), vmem(((KERN + 1) // 2, width), F32)
    padded = vmem((2, rows + HALO, width), F32)
    per_peer = dma((n,))
    return pl.pallas_call(
        layer_kernel,
        out_shape=[
            shape((rows, width), BF),
            shape((n, rows, 128), BF),
            shape((n, half, 128), BF),
            shape((width, width), BF),
            shape((KERN + 1, width), F32),
        ],
        in_specs=[SM] + [ANY] * 6,
        out_specs=[ANY] * 5,
        scratch_shapes=[
            frames, frames, frames, square, frames, vmem((KERN, width), F32),
            frames, wide, narrow, square, taps_all,
            frames, vmem((width // 2, width), BF), taps_half,
            lanes, lanes, lanes, vmem((HD, total), BF),
            vmem((SUB, total, BLK), F32), vmem((total // BLK, total, BLK), BF),
            vmem((total, 128), F32), narrow, dma((6,)), dma((5,)),
            wide, narrow, wide, narrow, vmem((HD + 16, total), BF), narrow, narrow,
            *[per_peer] * 6,
            square, taps_all, vmem((width // 2, width), BF), taps_half,
            frames, vmem((HALO, width), BF), padded,
            vmem((rows, width), F32), vmem((HALO, width), BF), padded,
            frames, narrow,
            dma, dma, dma, dma, per_peer, per_peer, dma((2,)), dma((2,)),
            *bufs, *sems,
            lanes, lanes, vmem((HD, total), F32), wide, narrow,
            *[per_peer] * 4,
        ],
        compiler_params=pltpu.CompilerParams(
            collective_id=0, has_side_effects=True, vmem_limit_bytes=62 * 2**20 - 2**19
        ),
        name="layer",
    )(starts, q, k, v, weight, cot, taps)


def finish_kernel(
    factor, kv_ref, q_ref, layer_ref, w_ref, conv_ref, layer_out, dq_out, dk_out, dv_out, w_out, conv_out
):
    rows = kv_ref.shape[1]
    half = rows // 2
    low = low_lanes(rows)
    for t in range(kv_ref.shape[0] // 2):
        cut = slice(t * 128, (t + 1) * 128)
        one, two = kv_ref[2 * t].astype(F32), kv_ref[2 * t + 1].astype(F32)
        dk_out[:, cut] = jnp.where(low, one, swap(two)).astype(BF)
        dv_out[:, cut] = jnp.where(low, swap(one), two).astype(BF)
        top, bottom = unpack_halves(q_ref[2 * t].astype(F32), q_ref[2 * t + 1].astype(F32))
        dq_out[0:half, cut] = top.astype(BF)
        dq_out[half:rows, cut] = bottom.astype(BF)
    layer_out[...] = layer_ref[...]
    w_out[...] = w_ref[...].astype(F32) * factor
    conv_out[...] = conv_ref[0:KERN, :] * factor


def finish(kv, q, layer, w_sum, conv_sum, factor):
    rows, width = layer.shape
    steps = STEPS
    wide, heads = width // steps, width // HD // steps
    shape = jax.ShapeDtypeStruct
    column = pl.BlockSpec((rows, wide), lambda t: (0, t))
    band = pl.BlockSpec((wide, width), lambda t: (t, 0))
    return pl.pallas_call(
        functools.partial(finish_kernel, factor),
        grid=(steps,),
        out_shape=[shape((rows, width), BF)] * 4
        + [shape((width, width), F32), shape((KERN, width), F32)],
        in_specs=[
            pl.BlockSpec((heads, rows, 128), lambda t: (t, 0, 0)),
            pl.BlockSpec((heads, rows // 2, 128), lambda t: (t, 0, 0)),
            column,
            band,
            pl.BlockSpec((KERN + 1, wide), lambda t: (0, t)),
        ],
        out_specs=[column] * 4 + [band, pl.BlockSpec((KERN, wide), lambda t: (0, t))],
        name="finish",
    )(kv, q, layer, w_sum, conv_sum)


def reducer(sums, conv_sums, w_out, conv_out, bufs, sems):
    two, mine, three, part, four, conv_two, conv_three, conv_part = bufs
    s2, r2, s3, r3, s4, r4, s5, r5, s6, r6 = sems
    n, groups = lax.axis_size("seq"), lax.axis_size("dp")
    me, dp = lax.axis_index("seq"), lax.axis_index("dp")
    width = w_out.shape[0]
    core, z = lax.rem(me, 2), me // 2
    deep = n // 2
    half = width // 2
    blk = half // groups
    lanes = width // deep
    conv_half = (KERN + 1) // 2
    per_row = groups // 2
    conv_lanes = width // per_row
    sibling = me + 1 - 2 * core

    def send(src, dst, ss, rs, dev):
        return pltpu.make_async_remote_copy(
            src_ref=src, dst_ref=dst, send_sem=ss, recv_sem=rs, device_id=dev
        )

    def tile(ref, index, first=0):
        row = pl.multiple_of(first + 8 * (index // per_row), 8)
        return ref.at[pl.ds(row, 8), rows_at(lax.rem(index, per_row), conv_lanes)]

    def c2(peer, owner, dev):
        dev = {"dp": dev}
        return (
            send(sums.at[rows_at(peer, blk), :], two.at[owner], s2.at[0, peer], r2.at[0, owner], dev),
            send(tile(conv_sums, peer), conv_two.at[owner], s2.at[1, peer], r2.at[1, owner], dev),
        )

    def c3(peer, owner, dev):
        dev = {"seq": dev * 2 + core}
        return (
            send(mine.at[:, rows_at(peer, lanes)], three.at[owner], s3.at[0, peer], r3.at[0, owner], dev),
            send(conv_part, conv_three.at[owner], s3.at[1, peer], r3.at[1, owner], dev),
        )

    def c4(peer, owner, dev):
        dev = {"seq": dev * 2 + core}
        return (send(part, four.at[:, rows_at(owner, lanes)], s4.at[peer], r4.at[owner], dev),)

    def c5(peer, owner, dev):
        dev = {"dp": dev}
        to = w_out.at[rows_at(core * groups + owner, blk), :]
        return (
            send(four, to, s5.at[0, peer], r5.at[0, owner], dev),
            send(conv_part, tile(conv_out, owner, core * conv_half), s5.at[1, peer], r5.at[1, owner], dev),
        )

    def c6(owner):
        dev = {"seq": sibling}
        here, there = w_out.at[rows_at(owner, half), :], conv_out.at[rows_at(owner, conv_half), :]
        return send(here, here, s6.at[0], r6.at[0], dev), send(there, there, s6.at[1], r6.at[1], dev)

    def to_all(copies, own, count):
        def go(d, _):
            peer = lax.rem(own + d, count)
            for copy in copies(peer, own, peer):
                copy.start()
            return 0

        lax.fori_loop(1, count, go, 0)

    def from_all(copies, own, count):
        def go(d, _):
            for copy in copies(own, lax.rem(own - d + count, count), own):
                copy.wait_recv()
            return 0

        lax.fori_loop(1, count, go, 0)

    def step1():
        to_all(c2, dp, groups)

    def step2():
        from_all(c2, dp, groups)
        two[dp] = sums[rows_at(dp, blk), :]
        conv_two[dp] = tile(conv_sums, dp)[...]

        def add(i, total):
            return total[0] + two[i].astype(F32), total[1] + conv_two[i]

        zero = jnp.zeros((blk, width), F32), jnp.zeros((8, conv_lanes), F32)
        total = lax.fori_loop(0, groups, add, zero)
        mine[...] = total[0].astype(BF)
        conv_part[...] = total[1]
        to_all(c3, z, deep)

    def step3():
        from_all(c3, z, deep)
        three[z] = mine[:, rows_at(z, lanes)]
        conv_three[z] = conv_part[...]
        total, conv_total = jnp.zeros((blk, lanes), F32), jnp.zeros((8, conv_lanes), F32)
        for i in range(deep):
            total = total + three[i].astype(F32)
            conv_total = conv_total + conv_three[i]
        part[...] = total.astype(BF)
        four[:, rows_at(z, lanes)] = part[...]

        def settle(d, _):
            c3(lax.rem(z + d, deep), z, lax.rem(z + d, deep))[1].wait_send()
            return 0

        lax.fori_loop(1, deep, settle, 0)
        conv_part[...] = conv_total
        to_all(c4, z, deep)

    def step4():
        from_all(c4, z, deep)
        w_out[rows_at(core * groups + dp, blk), :] = four[...]
        tile(conv_out, dp, core * conv_half)[...] = conv_part[...]
        to_all(c5, dp, groups)

    def step5():
        from_all(c5, dp, groups)
        for copy in c6(core):
            copy.start()

    def step6():
        for copy in c6(1 - core):
            copy.wait_recv()
        for copy in c6(core):
            copy.wait_send()

        def settle_dp(d, _):
            peer = lax.rem(dp + d, groups)
            for copy in (*c2(peer, dp, peer), *c5(peer, dp, peer)):
                copy.wait_send()
            return 0

        lax.fori_loop(1, groups, settle_dp, 0)

        def settle_z(d, _):
            peer = lax.rem(z + d, deep)
            for copy in (c3(peer, z, peer)[0], *c4(peer, z, peer)):
                copy.wait_send()
            return 0

        lax.fori_loop(1, deep, settle_z, 0)

    return step1, step2, step3, step4, step5, step6


def reducer_bufs(width, n, groups):
    half, deep = width // 2, n // 2
    blk, lanes = half // groups, width // deep
    conv_lanes = width // (groups // 2)
    dma = pltpu.SemaphoreType.DMA
    bufs = [
        pltpu.VMEM((groups, blk, width), BF),
        pltpu.VMEM((blk, width), BF),
        pltpu.VMEM((deep, blk, lanes), BF),
        pltpu.VMEM((blk, lanes), BF),
        pltpu.VMEM((blk, width), BF),
        pltpu.VMEM((groups, 8, conv_lanes), F32),
        pltpu.VMEM((deep, 8, conv_lanes), F32),
        pltpu.VMEM((8, conv_lanes), F32),
    ]
    sems = [dma((2, groups))] * 2 + [dma((2, deep))] * 2 + [dma((deep,))] * 2
    sems += [dma((2, groups))] * 2 + [dma((2,))] * 2
    return bufs, sems


def local(query_proj, key_proj, value_proj, cotangent, out_weight, conv_weight, rec_starts):
    rows, width = query_proj.shape[1:]
    factor = (lax.axis_size("dp") * lax.axis_size("seq") * rows) ** -0.5
    out, kv, q, weight_sum, conv_sum = layer(
        rec_starts, query_proj[0], key_proj[0], value_proj[0], out_weight, cotangent[0], conv_weight
    )
    out, dq, dk, dv, weight_grad, conv_grad = finish(kv, q, out, weight_sum, conv_sum, factor)
    return out[None], dq[None], dk[None], dv[None], weight_grad, conv_grad


def solution(mesh):
    frames = P("dp", "seq", None)
    return jax.shard_map(
        local,
        mesh=mesh,
        in_specs=(frames, frames, frames, frames, P(), P(), P("dp", None)),
        out_specs=(frames, frames, frames, frames, P(), P()),
        check_vma=False,
    )
```

```python
import functools

import jax
import jax.numpy as jnp
from jax import lax
from jax.experimental import pallas as pl
from jax.experimental.pallas import tpu as pltpu
from jax.sharding import PartitionSpec as P

HD = 64
KERN = 31
HALO = 32
BLK = 256
SUB = 3
STEPS = 2
BIG = 1e30
BF = jnp.bfloat16
F32 = jnp.float32
VM = pl.BlockSpec(memory_space=pltpu.VMEM)
SM = pl.BlockSpec(memory_space=pltpu.SMEM)
ANY = pl.BlockSpec(memory_space=pl.ANY)


def dot(a, b, ca=1, cb=0):
    return lax.dot_general(a, b, (((ca,), (cb,)), ((), ())), preferred_element_type=F32)


def low_lanes(rows):
    return lax.broadcasted_iota(jnp.int32, (rows, 128), 1) < HD


def swap(x):
    return pltpu.roll(x, HD, 1)


def pack_halves(x):
    half = x.shape[0] // 2
    low = low_lanes(half)
    top, bottom = x[:half], x[half:]
    return jnp.where(low, top, swap(bottom)), jnp.where(low, swap(top), bottom)


def unpack_halves(first, second):
    low = low_lanes(first.shape[0])
    return jnp.where(low, first, swap(second)), jnp.where(low, swap(first), second)


def greet(axes):
    barrier = pltpu.get_barrier_semaphore()
    total = 0
    for axis in axes:
        count = lax.axis_size(axis)
        me = lax.axis_index(axis)

        def signal(d, _, axis=axis, count=count, me=me):
            pl.semaphore_signal(barrier, inc=1, device_id={axis: lax.rem(me + d, count)})
            return 0

        lax.fori_loop(1, count, signal, 0)
        total += count - 1
    return total


def ring_order(n):
    deep = n // 2
    order = []
    for far in range(deep // 2 - 1, 1, -1):
        order += [(far, 0), (-far, 0), (far, 1), (-far, 1)]
    order += [(deep // 2, 0), (0, 1), (deep // 2, 1), (0, 0)]
    return order + [(1, 0), (-1, 0), (1, 1), (-1, 1)]


def slot_owners(n):
    me = lax.axis_index("seq")
    core, z = lax.rem(me, 2), me // 2
    deep = n // 2
    owners = []
    for steps, other in ring_order(n):
        owner = 2 * lax.rem(z + (steps + deep) % deep, deep) + (1 - core if other else core)
        owners.append((owner, steps == 0 and not other))
    return owners


def rows_at(index, size):
    return pl.ds(pl.multiple_of(index * size, size), size)


def attend(
    starts, q_ref, k_ref, v_ref, loads, greeted, mixed_out,
    qk_send, v_send, qk_recv, v_recv, kx, qx, vx, kt, vt, s_buf, p_buf, aux, mix_send, mix_recv,
    k_ss, k_rs, v_ss, v_rs, m_ss, m_rs,
):
    n = lax.axis_size("seq")
    me = lax.axis_index("seq")
    rows, width = q_ref.shape
    half = rows // 2
    total = n * rows
    chunks = total // BLK
    group = SUB * BLK
    groups = total // group
    early = groups // 2
    owners = group // rows
    slots = slot_owners(n)
    for load in loads[:2]:
        load.wait()
    for t in range(width // 128):
        cols = pl.ds(t * 128, 128)
        q_, k_ = q_ref[:, cols].astype(F32) * (HD**-0.5), k_ref[:, cols].astype(F32)
        low = low_lanes(rows)
        qk_send[2 * t] = jnp.where(low, q_, swap(k_)).astype(BF)
        qk_send[2 * t + 1] = jnp.where(low, swap(q_), k_).astype(BF)
    pl.semaphore_wait(pltpu.get_barrier_semaphore(), greeted)

    def qk_copy(peer, owner, dst_dev):
        return pltpu.make_async_remote_copy(
            src_ref=qk_send.at[peer],
            dst_ref=qk_recv.at[owner],
            send_sem=k_ss.at[peer],
            recv_sem=k_rs.at[owner],
            device_id={"seq": dst_dev},
        )

    def v_copy(peer, owner, dst_dev):
        return pltpu.make_async_remote_copy(
            src_ref=v_send.at[peer],
            dst_ref=v_recv.at[owner],
            send_sem=v_ss.at[peer],
            recv_sem=v_rs.at[owner],
            device_id={"seq": dst_dev},
        )

    for peer, own in slots:
        if not own:
            qk_copy(peer, me, peer).start()
    loads[2].wait()
    for t in range(width // 128):
        first, second = pack_halves(v_ref[:, t * 128 : (t + 1) * 128].astype(F32))
        v_send[2 * t] = first.astype(BF)
        v_send[2 * t + 1] = second.astype(BF)
    for peer, own in slots:
        if not own:
            v_copy(peer, me, peer).start()
    second = starts[0, 1]

    def take_qk(slot, src):
        at = lax.broadcasted_iota(jnp.int32, (rows, 128), 0) + src * rows
        lane = lax.broadcasted_iota(jnp.int32, (rows, 128), 1) - HD
        later = jnp.where(at >= second, 1.0, 0.0)
        own = jnp.where(lane == 0, 1.0 - later, jnp.where(lane == 1, later, 0.0))
        other = jnp.where(lane == 0, later, jnp.where(lane == 1, 1.0 - later, 0.0)) * (-BIG)
        x = qk_recv[src].astype(F32)
        qx[slot * rows : (slot + 1) * rows, :] = jnp.where(lane < 0, x, own).astype(BF)
        kx[slot * rows : (slot + 1) * rows, :] = jnp.where(lane < 0, swap(x), other).astype(BF)

    qk_recv[me] = qk_send[me]
    for slot, (src, own) in enumerate(slots):
        if not own:
            qk_copy(me, src, me).wait_recv()
        take_qk(slot, src)

    def scores(c, q_blk):
        return dot(kx[c * BLK : (c + 1) * BLK, :], q_blk, 1, 1)

    def col_max(best, s):
        return jnp.maximum(best, jnp.max(s.reshape(BLK // 8, 8, BLK), axis=0))

    low_start = jnp.full((8, BLK), -3e38, F32)
    q_blk = qx[0:BLK, :]
    best = low_start
    for c in range(chunks):
        s = scores(c, q_blk)
        s_buf[0, c * BLK : (c + 1) * BLK, :] = s
        best = col_max(best, s)

    def mix_copy(peer, owner, dst_dev):
        return pltpu.make_async_remote_copy(
            src_ref=mix_send.at[peer],
            dst_ref=mix_recv.at[owner],
            send_sem=m_ss.at[peer],
            recv_sem=m_rs.at[owner],
            device_id={"seq": dst_dev},
        )

    def finish_block(at, acc):
        inverse = 1.0 / acc[HD : HD + 1]
        mixed = (acc[:HD] * inverse).astype(BF).astype(F32)
        both = jnp.concatenate([jnp.broadcast_to(inverse, (HD, BLK)), mixed], axis=0)
        aux[rows_at(at, BLK), :] = both.T

    def send_some(g):
        for slot in range(g * owners, (g + 1) * owners):
            owner, own = slots[slot]
            top = aux[slot * rows : slot * rows + half, :]
            bottom = aux[slot * rows + half : (slot + 1) * rows, :]
            mix_send[owner] = jnp.where(low_lanes(half), swap(top), bottom).astype(BF)
            if own:
                mix_recv[owner] = mix_send[owner]
            else:
                mix_copy(owner, me, owner).start()

    def send_group(i):
        for g in range(groups):
            pl.when(i == g)(functools.partial(send_some, g))

    def one_group(i, m, with_values):
        g = i
        g_next = lax.rem(i + 1, groups)
        for sub in range(SUB):
            at = g * SUB + sub
            ahead = (sub + 1) % SUB
            next_at = at + 1 if sub + 1 < SUB else g_next * SUB
            q_next = qx[rows_at(next_at, BLK), :]
            best = low_start
            acc = jnp.zeros((HD + 16, BLK), F32)
            for c in range(chunks):
                cut = slice(c * BLK, (c + 1) * BLK)
                s = scores(c, q_next)
                s_buf[ahead, cut, :] = s
                best = col_max(best, s)
                p = jnp.exp(s_buf[sub, cut, :] - m).astype(BF)
                p_buf[at, cut, :] = p
                if with_values:
                    acc = acc + dot(vt[:, cut], p)
            m = jnp.max(best, axis=0, keepdims=True)
            if with_values:
                finish_block(at, acc)
        if with_values:
            send_group(g)
        return m

    m = lax.fori_loop(
        0, early, functools.partial(one_group, with_values=False), jnp.max(best, axis=0, keepdims=True)
    )
    v_recv[me] = v_send[me]
    lane = lax.broadcasted_iota(jnp.int32, (half, 128), 1) - HD
    ones = jnp.where((lane >= 0) & (lane < 3), 1.0, 0.0)
    for slot, (src, own) in enumerate(slots):
        if not own:
            v_copy(me, src, me).wait_recv()
        x = v_recv[src].astype(F32)
        at = slot * rows
        vx[at : at + half, :] = jnp.where(lane < 0, x, ones).astype(BF)
        vx[at + half : at + rows, :] = jnp.where(lane < 0, swap(x), ones).astype(BF)
    vt[HD : HD + 16, :] = jnp.ones((16, total), BF)
    for c in range(chunks):
        cut = slice(c * BLK, (c + 1) * BLK)
        vt[0:HD, cut] = vx[cut, :].T[:HD]

    def late_values(i, _):
        g = i
        for sub in range(SUB):
            acc = jnp.zeros((HD + 16, BLK), F32)
            for c in range(chunks):
                cut = slice(c * BLK, (c + 1) * BLK)
                acc = acc + dot(vt[:, cut], p_buf[g * SUB + sub, cut, :])
            finish_block(g * SUB + sub, acc)
        send_group(g)
        return 0

    lax.fori_loop(0, early, late_values, 0)
    lax.fori_loop(early, groups, functools.partial(one_group, with_values=True), m)
    for c in range(chunks):
        cut = slice(c * BLK, (c + 1) * BLK)
        kt[:, cut] = kx[cut, :].T[:HD]
    def settle(d, _):
        peer = lax.rem(me + d, n)
        qk_copy(peer, me, peer).wait_send()
        v_copy(peer, me, peer).wait_send()
        mix_copy(peer, me, peer).wait_send()
        mix_copy(me, lax.rem(me - d + n, n), me).wait_recv()
        return 0

    lax.fori_loop(1, n, settle, 0)
    for t in range(width // 128):
        top, bottom = unpack_halves(mix_recv[2 * t].astype(F32), mix_recv[2 * t + 1].astype(F32))
        mixed_out[0:half, t * 128 : (t + 1) * 128] = top.astype(BF)
        mixed_out[half:rows, t * 128 : (t + 1) * 128] = bottom.astype(BF)


def convolve(
    starts, mixed_ref, w_ref, cot_ref, taps_ref, layer_out, sums_out, csums_out, start_reduction,
    wpart, cpart, one, conv_one, proj, halo_recv, pad, head, ahead_recv, cpad, pb, back_send, back_recv,
    h_ss, h_rs, a_ss, a_rs, b_ss, b_rs, c_ss, c_rs,
):
    n = lax.axis_size("seq")
    me = lax.axis_index("seq")
    rows, width = mixed_ref.shape
    groups = rows // 8
    edge = HALO // 8
    total = n * rows
    second = starts[0, 1]
    base = me * rows
    right, left = lax.rem(me + 1, n), lax.rem(me + n - 1, n)
    step = 256
    for t in range(width // step):
        cut = pl.ds(t * step, step)
        out = dot(mixed_ref[...], w_ref[:, cut]).astype(BF)
        proj[:, cut] = out
        pad[0, HALO : HALO + rows, cut] = out.astype(F32)
    halo = pltpu.make_async_remote_copy(
        src_ref=proj.at[pl.ds(rows - HALO, HALO)],
        dst_ref=halo_recv,
        send_sem=h_ss,
        recv_sem=h_rs,
        device_id={"seq": right},
    )
    halo.start()

    def frame(first, count):
        return lax.broadcasted_iota(jnp.int32, (count, width), 0) + first

    pad[1, HALO : HALO + rows, :] = jnp.where(
        frame(base, rows) >= second, pad[0, HALO : HALO + rows, :], 0.0
    )

    def later(g):
        return (base + 8 * g >= second).astype(jnp.int32)

    def conv_groups(which):
        def one_tile(t, _):
            cut = rows_at(t, 128)
            w = [jnp.broadcast_to(taps_ref[j : j + 1, cut], (8, 128)) for j in range(KERN)]
            for g in which:
                acc = jnp.zeros((8, 128), F32)
                lab = later(g)
                for j in range(KERN):
                    acc = acc + w[j] * pad[lab, 8 * g + j + 2 : 8 * g + j + 10, cut]
                gate = jax.nn.sigmoid(acc)
                here = slice(8 * g, 8 * g + 8)
                layer = pad[0, HALO + 8 * g : HALO + 8 * g + 8, cut] + acc * gate
                head[here, cut] = layer
                cot = cot_ref[here, cut].astype(F32)
                back = cot * (gate * (1.0 + acc * (1.0 - gate)))
                cpad[1, here, cut] = back
                cpad[0, here, cut] = jnp.where(base + 8 * g < second, back, 0.0)
            return 0

        lax.fori_loop(0, width // 128, one_tile, 0)

    conv_groups(range(edge, groups))
    halo.wait_recv()
    before = halo_recv[...].astype(F32)
    pad[0, 0:HALO, :] = jnp.where(me > 0, before, 0.0)
    pad[1, 0:HALO, :] = jnp.where(
        (frame(base - HALO, HALO) >= second) & (me > 0), before, 0.0
    )
    conv_groups(range(edge))
    pb[0:HALO, :] = cpad[1, 0:HALO, :].astype(BF)
    ahead = pltpu.make_async_remote_copy(
        src_ref=pb.at[pl.ds(0, HALO)],
        dst_ref=ahead_recv,
        send_sem=a_ss,
        recv_sem=a_rs,
        device_id={"seq": left},
    )
    ahead.start()
    layer_out[...] = head[...].astype(BF)

    def spread_groups(which):
        def one_tile(t, _):
            cut = rows_at(t, 128)
            w = [jnp.broadcast_to(taps_ref[j : j + 1, cut], (8, 128)) for j in range(KERN)]
            for g in which:
                acc = cot_ref[8 * g : 8 * g + 8, cut].astype(F32)
                lab = later(g)
                for j in range(KERN):
                    acc = acc + w[j] * cpad[lab, 8 * g + 30 - j : 8 * g + 38 - j, cut]
                head[8 * g : 8 * g + 8, cut] = acc
            return 0

        lax.fori_loop(0, width // 128, one_tile, 0)

    spread_groups(range(groups - edge))
    ahead.wait()
    after = ahead_recv[...].astype(F32)
    inside = me < n - 1
    cpad[1, rows : rows + HALO, :] = jnp.where(inside, after, 0.0)
    cpad[0, rows : rows + HALO, :] = jnp.where(
        (frame(base + rows, HALO) < second) & inside, after, 0.0
    )
    spread_groups(range(groups - edge, groups))
    pb[...] = head[...].astype(BF)
    for t in range(width // step):
        out = dot(pb[...], w_ref[t * step : (t + 1) * step, :], 1, 1).astype(BF).astype(F32)
        for u in range(step // 128):
            first, second_ = pack_halves(out[:, u * 128 : (u + 1) * 128])
            at = 2 * (t * (step // 128) + u)
            back_send[at] = first.astype(BF)
            back_send[at + 1] = second_.astype(BF)

    def back_copy(peer, owner, dst_dev):
        return pltpu.make_async_remote_copy(
            src_ref=back_send.at[peer],
            dst_ref=back_recv.at[owner],
            send_sem=b_ss.at[peer],
            recv_sem=b_rs.at[owner],
            device_id={"seq": dst_dev},
        )

    for peer, own in slot_owners(n):
        if not own:
            back_copy(peer, me, peer).start()
    back_recv[me] = back_send[me]
    for t in range(width // step):
        cut = pl.ds(t * step, step)
        wpart[cut, :] = dot(mixed_ref[:, cut], pb[...], 0, 0).astype(BF)
    core = lax.rem(me, 2)
    sibling = me + 1 - 2 * core
    part, conv_part = width // 2, (KERN + 1) // 2
    pair = pltpu.make_async_remote_copy(
        src_ref=wpart.at[rows_at(1 - core, part), :],
        dst_ref=one,
        send_sem=c_ss.at[0],
        recv_sem=c_rs.at[0],
        device_id={"seq": sibling},
    )
    pair.start()

    def tap_tile(t, _):
        cut = rows_at(t, 128)
        acc = [jnp.zeros((8, 128), F32)] * KERN
        for g in range(groups):
            lab = later(g)
            signal = cpad[1, 8 * g : 8 * g + 8, cut]
            for j in range(KERN):
                acc[j] = acc[j] + signal * pad[lab, 8 * g + j + 2 : 8 * g + j + 10, cut]
        for j in range(KERN):
            cpart[j : j + 1, cut] = jnp.sum(acc[j], axis=0, keepdims=True)
        cpart[KERN:, cut] = jnp.zeros((1, 128), F32)
        return 0

    lax.fori_loop(0, width // 128, tap_tile, 0)
    conv_pair = pltpu.make_async_remote_copy(
        src_ref=cpart.at[rows_at(1 - core, conv_part), :],
        dst_ref=conv_one,
        send_sem=c_ss.at[1],
        recv_sem=c_rs.at[1],
        device_id={"seq": sibling},
    )
    conv_pair.start()
    pair.wait()

    def add(i, _):
        own = wpart[pl.ds(pl.multiple_of(core * part + i * 32, 32), 32), :].astype(F32)
        sums_out[rows_at(i, 32), :] = (own + one[rows_at(i, 32), :].astype(F32)).astype(BF)
        return 0

    lax.fori_loop(0, part // 32, add, 0)
    conv_pair.wait()
    csums_out[...] = cpart[rows_at(core, conv_part), :] + conv_one[...]
    start_reduction()
    halo.wait_send()

    def arrived(src):
        back_copy(me, src, me).wait_recv()

    def settle(d, _):
        peer = lax.rem(me + d, n)
        back_copy(peer, me, peer).wait_send()
        return 0

    return arrived, lambda: lax.fori_loop(1, n, settle, 0)


def attend_back(
    p_buf, vx, qx, kt, aux, back, arrived, kv_recv, q_recv, copies, steps,
    of, qd, s_buf, dqt, kv_send, q_send, kv_ss, kv_rs, q_ss, q_rs,
):
    n = lax.axis_size("seq")
    me = lax.axis_index("seq")
    rows = kv_recv.shape[1]
    half = rows // 2
    total = n * rows
    chunks = total // BLK
    group = SUB * BLK
    groups = total // group
    owners = group // rows
    slots = slot_owners(n)

    def prepare(slot, src):
        x = back[src].astype(F32)
        low = low_lanes(half)
        lane = lax.broadcasted_iota(jnp.int32, (half, 128), 1) - HD
        for side in range(2):
            at = slice(slot * rows + side * half, slot * rows + (side + 1) * half)
            side_aux = aux[at, :]
            got = jnp.where(low, (x if side == 0 else swap(x)) * side_aux, 0.0)
            got = got.astype(BF).astype(F32)
            delta = -jnp.sum(got * swap(side_aux), axis=1, keepdims=True)
            top = delta.astype(BF).astype(F32)
            mid = (delta - top).astype(BF).astype(F32)
            rest = delta - top - mid
            feat = jnp.where(
                lane == 0, top, jnp.where(lane == 1, mid, jnp.where(lane == 2, rest, 0.0))
            )
            of[at, :] = jnp.where(low, got, feat).astype(BF)
            qd[at, :] = jnp.where(low, qx[at, :].astype(F32), swap(got)).astype(BF)

    dqt[...] = jnp.zeros_like(dqt)
    for slot, (src, own) in enumerate(slots):
        if not own:
            arrived(src)
        prepare(slot, src)
    places = {2: 1, 4: 2, 5: 3} if groups >= 4 else {0: 1, 1: 2, 2: 3}
    acc_k, acc_v = s_buf.at[1, 0:group, 0:128], s_buf.at[1, 0:group, 128:256]
    halves = chunks % 4 == 0

    def kv_copy(peer, owner, dst_dev):
        return pltpu.make_async_remote_copy(
            src_ref=kv_send.at[peer],
            dst_ref=kv_recv.at[owner],
            send_sem=kv_ss.at[peer],
            recv_sem=kv_rs.at[owner],
            device_id={"seq": dst_dev},
        )

    def q_copy(peer, owner, dst_dev):
        return pltpu.make_async_remote_copy(
            src_ref=q_send.at[peer],
            dst_ref=q_recv.at[owner],
            send_sem=q_ss.at[peer],
            recv_sem=q_rs.at[owner],
            device_id={"seq": dst_dev},
        )

    def send_q(side):
        def turn(j, _):
            c = j
            x = dqt[:, rows_at(c, BLK)] * (HD**-0.5)
            aux[rows_at(c, BLK), :] = jnp.concatenate([x, jnp.zeros_like(x)], axis=0).T
            return 0

        lax.fori_loop(side * chunks // 2, (side + 1) * chunks // 2, turn, 0)

        for slot in range(side * n // 2, (side + 1) * n // 2):
            owner, own = slots[slot]
            top = aux[slot * rows : slot * rows + half, :]
            bottom = aux[slot * rows + half : (slot + 1) * rows, :]
            q_send[owner] = jnp.where(low_lanes(half), top, swap(bottom)).astype(BF)
            if own:
                q_recv[owner] = q_send[owner]
            else:
                q_copy(owner, me, owner).start()

    def send_kv(g):
        for w in range(owners):
            owner, own = slots[g * owners + w]
            cut = slice(w * rows, (w + 1) * rows)
            kv_send[owner] = jnp.where(low_lanes(rows), acc_k[cut, :], acc_v[cut, :]).astype(BF)
            if own:
                kv_recv[owner] = kv_send[owner]
            else:
                kv_copy(owner, me, owner).start()

    def hooks(i, h):
        for place, number in places.items():
            if place % 2 == h:
                pl.when(i == place // 2)(steps[number])

    def one_group(i, _):
        g = i
        acc_k[...] = jnp.zeros_like(acc_k)
        acc_v[...] = jnp.zeros_like(acc_v)

        def prob_back(r, c):
            return dot(vx[rows_at(g * SUB + r, BLK), :], of[rows_at(c, BLK), :], 1, 1)

        for r in range(SUB):
            s_buf[0, r * BLK : (r + 1) * BLK, :] = prob_back(r, 0)

        def two_chunks(pair, _):
            for par in range(2):
                c = 2 * pair + par
                ahead = lax.rem(c + 1, chunks)
                q_d = qd[rows_at(c, BLK), :]
                dq = jnp.zeros((HD, BLK), F32)
                for r in range(SUB):
                    cut = slice(r * BLK, (r + 1) * BLK)
                    keys = rows_at(g * SUB + r, BLK)
                    there = slice((1 - par) * group + r * BLK, (1 - par) * group + (r + 1) * BLK)
                    here = slice(par * group + r * BLK, par * group + (r + 1) * BLK)
                    s_buf[0, there, :] = prob_back(r, ahead)
                    p = p_buf[c, keys, :]
                    ds = (p.astype(F32) * s_buf[0, here, :]).astype(BF)
                    acc_v[cut, :] += dot(p, q_d)
                    acc_k[cut, :] += dot(ds, q_d)
                    dq = dq + dot(kt[:, keys], ds)
                dqt[:, rows_at(c, BLK)] += dq
            return 0

        for h in range(2):
            lax.fori_loop(h * chunks // 4, (h + 1) * chunks // 4, two_chunks, 0)
            if h == 0:
                hooks(i, h)
                if halves:
                    pl.when(i == groups - 1)(functools.partial(send_q, 0))
        for group_at in range(groups):
            pl.when(i == group_at)(functools.partial(send_kv, group_at))
        hooks(i, 1)
        return 0

    lax.fori_loop(0, groups, one_group, 0)
    for side in range(1 if halves else 0, 2):
        send_q(side)

    steps[4]()

    def settle_kv(d, _):
        peer = lax.rem(me + d, n)
        kv_copy(peer, me, peer).wait_send()
        kv_copy(me, lax.rem(me - d + n, n), me).wait_recv()
        return 0

    lax.fori_loop(1, n, settle_kv, 0)
    copies[2].start()

    def settle_q(d, _):
        peer = lax.rem(me + d, n)
        q_copy(peer, me, peer).wait_send()
        q_copy(me, lax.rem(me - d + n, n), me).wait_recv()
        return 0

    lax.fori_loop(1, n, settle_q, 0)
    copies[3].start()
    steps[5]()
    copies[0].start()
    copies[1].start()


def layer_kernel(
    starts, q_hbm, k_hbm, v_hbm, w_hbm, cot_hbm, taps_hbm,
    layer_hbm, kv_hbm, qg_hbm, w_out_hbm, conv_hbm,
    q_ref, k_ref, v_ref, w_ref, cot_ref, taps_ref, layer_out, kv_recv, q_recv, w_out, conv_out,
    mixed, sums, conv_sums, kx, qx, vx, kt, s_buf, p_buf, aux, back_recv, in_sem, out_sem, *rest,
):
    rest = list(rest)

    def take(count):
        taken = rest[:count]
        del rest[:count]
        return taken

    greeted = greet(("seq", "dp"))
    sources = (q_hbm, k_hbm, v_hbm, w_hbm, cot_hbm, taps_hbm)
    places = (q_ref, k_ref, v_ref, w_ref, cot_ref, taps_ref)
    loads = [
        pltpu.make_async_copy(source, place, in_sem.at[i])
        for i, (source, place) in enumerate(zip(sources, places))
    ]
    for load in loads:
        load.start()
    results = ((w_out, w_out_hbm), (conv_out, conv_hbm), (kv_recv, kv_hbm), (q_recv, qg_hbm), (layer_out, layer_hbm))
    copies = [
        pltpu.make_async_copy(source, place, out_sem.at[i]) for i, (source, place) in enumerate(results)
    ]
    qk_send, v_send, qk_recv, v_recv, vt, mix_send, mix_recv = take(7)
    attend(
        starts, q_ref, k_ref, v_ref, loads, greeted, mixed,
        qk_send, v_send, qk_recv, v_recv, kx, qx, vx, kt, vt, s_buf, p_buf, aux, mix_send, mix_recv,
        *take(6),
    )
    for load in loads[3:]:
        load.wait()
    bufs = take(12)
    sems = take(8)
    reduce_bufs = take(8)
    steps = reducer(sums, conv_sums, w_out, conv_out, reduce_bufs, take(10))
    arrived, settle_back = convolve(
        starts, mixed, w_ref, cot_ref, taps_ref, layer_out, sums, conv_sums, steps[0],
        *bufs, back_recv, *sems,
    )
    copies[4].start()
    of, qd, dqt, kv_send, q_send = take(5)
    attend_back(
        p_buf, vx, qx, kt, aux, back_recv, arrived, kv_recv, q_recv, copies, steps,
        of, qd, s_buf, dqt, kv_send, q_send, *rest,
    )
    settle_back()
    for copy in copies:
        copy.wait()


def layer(starts, q, k, v, weight, cot, taps):
    rows, width = q.shape
    n, groups = lax.axis_size("seq"), lax.axis_size("dp")
    total, half = n * rows, rows // 2
    shape, vmem, dma = jax.ShapeDtypeStruct, pltpu.VMEM, pltpu.SemaphoreType.DMA
    bufs, sems = reducer_bufs(width, n, groups)
    wide, narrow, square = vmem((n, rows, 128), BF), vmem((n, half, 128), BF), vmem((width, width), BF)
    frames, lanes = vmem((rows, width), BF), vmem((total, 128), BF)
    taps_all, taps_half = vmem((KERN + 1, width), F32), vmem(((KERN + 1) // 2, width), F32)
    padded = vmem((2, rows + HALO, width), F32)
    per_peer = dma((n,))
    return pl.pallas_call(
        layer_kernel,
        out_shape=[
            shape((rows, width), BF),
            shape((n, rows, 128), BF),
            shape((n, half, 128), BF),
            shape((width, width), BF),
            shape((KERN + 1, width), F32),
        ],
        in_specs=[SM] + [ANY] * 6,
        out_specs=[ANY] * 5,
        scratch_shapes=[
            frames, frames, frames, square, frames, vmem((KERN, width), F32),
            frames, wide, narrow, square, taps_all,
            frames, vmem((width // 2, width), BF), taps_half,
            lanes, lanes, lanes, vmem((HD, total), BF),
            vmem((SUB, total, BLK), F32), vmem((total // BLK, total, BLK), BF),
            vmem((total, 128), F32), narrow, dma((6,)), dma((5,)),
            wide, narrow, wide, narrow, vmem((HD + 16, total), BF), narrow, narrow,
            *[per_peer] * 6,
            square, taps_all, vmem((width // 2, width), BF), taps_half,
            frames, vmem((HALO, width), BF), padded,
            vmem((rows, width), F32), vmem((HALO, width), BF), padded,
            frames, narrow,
            dma, dma, dma, dma, per_peer, per_peer, dma((2,)), dma((2,)),
            *bufs, *sems,
            lanes, lanes, vmem((HD, total), F32), wide, narrow,
            *[per_peer] * 4,
        ],
        compiler_params=pltpu.CompilerParams(
            collective_id=0, has_side_effects=True, vmem_limit_bytes=62 * 2**20 - 2**19
        ),
        name="layer",
    )(starts, q, k, v, weight, cot, taps)


def finish_kernel(
    factor, kv_ref, q_ref, layer_ref, w_ref, conv_ref, layer_out, dq_out, dk_out, dv_out, w_out, conv_out
):
    rows = kv_ref.shape[1]
    half = rows // 2
    low = low_lanes(rows)
    for t in range(kv_ref.shape[0] // 2):
        cut = slice(t * 128, (t + 1) * 128)
        one, two = kv_ref[2 * t].astype(F32), kv_ref[2 * t + 1].astype(F32)
        dk_out[:, cut] = jnp.where(low, one, swap(two)).astype(BF)
        dv_out[:, cut] = jnp.where(low, swap(one), two).astype(BF)
        top, bottom = unpack_halves(q_ref[2 * t].astype(F32), q_ref[2 * t + 1].astype(F32))
        dq_out[0:half, cut] = top.astype(BF)
        dq_out[half:rows, cut] = bottom.astype(BF)
    layer_out[...] = layer_ref[...]
    w_out[...] = w_ref[...].astype(F32) * factor
    conv_out[...] = conv_ref[0:KERN, :] * factor


def finish(kv, q, layer, w_sum, conv_sum, factor):
    rows, width = layer.shape
    steps = STEPS
    wide, heads = width // steps, width // HD // steps
    shape = jax.ShapeDtypeStruct
    column = pl.BlockSpec((rows, wide), lambda t: (0, t))
    band = pl.BlockSpec((wide, width), lambda t: (t, 0))
    return pl.pallas_call(
        functools.partial(finish_kernel, factor),
        grid=(steps,),
        out_shape=[shape((rows, width), BF)] * 4
        + [shape((width, width), F32), shape((KERN, width), F32)],
        in_specs=[
            pl.BlockSpec((heads, rows, 128), lambda t: (t, 0, 0)),
            pl.BlockSpec((heads, rows // 2, 128), lambda t: (t, 0, 0)),
            column,
            band,
            pl.BlockSpec((KERN + 1, wide), lambda t: (0, t)),
        ],
        out_specs=[column] * 4 + [band, pl.BlockSpec((KERN, wide), lambda t: (0, t))],
        name="finish",
    )(kv, q, layer, w_sum, conv_sum)


def reducer(sums, conv_sums, w_out, conv_out, bufs, sems):
    two, mine, three, part, four, conv_two, conv_three, conv_part = bufs
    s2, r2, s3, r3, s4, r4, s5, r5, s6, r6 = sems
    n, groups = lax.axis_size("seq"), lax.axis_size("dp")
    me, dp = lax.axis_index("seq"), lax.axis_index("dp")
    width = w_out.shape[0]
    core, z = lax.rem(me, 2), me // 2
    deep = n // 2
    half = width // 2
    blk = half // groups
    lanes = width // deep
    conv_half = (KERN + 1) // 2
    per_row = groups // 2
    conv_lanes = width // per_row
    sibling = me + 1 - 2 * core

    def send(src, dst, ss, rs, dev):
        return pltpu.make_async_remote_copy(
            src_ref=src, dst_ref=dst, send_sem=ss, recv_sem=rs, device_id=dev
        )

    def tile(ref, index, first=0):
        row = pl.multiple_of(first + 8 * (index // per_row), 8)
        return ref.at[pl.ds(row, 8), rows_at(lax.rem(index, per_row), conv_lanes)]

    def c2(peer, owner, dev):
        dev = {"dp": dev}
        return (
            send(sums.at[rows_at(peer, blk), :], two.at[owner], s2.at[0, peer], r2.at[0, owner], dev),
            send(tile(conv_sums, peer), conv_two.at[owner], s2.at[1, peer], r2.at[1, owner], dev),
        )

    def c3(peer, owner, dev):
        dev = {"seq": dev * 2 + core}
        return (
            send(mine.at[:, rows_at(peer, lanes)], three.at[owner], s3.at[0, peer], r3.at[0, owner], dev),
            send(conv_part, conv_three.at[owner], s3.at[1, peer], r3.at[1, owner], dev),
        )

    def c4(peer, owner, dev):
        dev = {"seq": dev * 2 + core}
        return (send(part, four.at[:, rows_at(owner, lanes)], s4.at[peer], r4.at[owner], dev),)

    def c5(peer, owner, dev):
        dev = {"dp": dev}
        to = w_out.at[rows_at(core * groups + owner, blk), :]
        return (
            send(four, to, s5.at[0, peer], r5.at[0, owner], dev),
            send(conv_part, tile(conv_out, owner, core * conv_half), s5.at[1, peer], r5.at[1, owner], dev),
        )

    def c6(owner):
        dev = {"seq": sibling}
        here, there = w_out.at[rows_at(owner, half), :], conv_out.at[rows_at(owner, conv_half), :]
        return send(here, here, s6.at[0], r6.at[0], dev), send(there, there, s6.at[1], r6.at[1], dev)

    def to_all(copies, own, count):
        def go(d, _):
            peer = lax.rem(own + d, count)
            for copy in copies(peer, own, peer):
                copy.start()
            return 0

        lax.fori_loop(1, count, go, 0)

    def from_all(copies, own, count):
        def go(d, _):
            for copy in copies(own, lax.rem(own - d + count, count), own):
                copy.wait_recv()
            return 0

        lax.fori_loop(1, count, go, 0)

    def step1():
        to_all(c2, dp, groups)

    def step2():
        from_all(c2, dp, groups)
        two[dp] = sums[rows_at(dp, blk), :]
        conv_two[dp] = tile(conv_sums, dp)[...]

        def add(i, total):
            return total[0] + two[i].astype(F32), total[1] + conv_two[i]

        zero = jnp.zeros((blk, width), F32), jnp.zeros((8, conv_lanes), F32)
        total = lax.fori_loop(0, groups, add, zero)
        mine[...] = total[0].astype(BF)
        conv_part[...] = total[1]
        to_all(c3, z, deep)

    def step3():
        from_all(c3, z, deep)
        three[z] = mine[:, rows_at(z, lanes)]
        conv_three[z] = conv_part[...]
        total, conv_total = jnp.zeros((blk, lanes), F32), jnp.zeros((8, conv_lanes), F32)
        for i in range(deep):
            total = total + three[i].astype(F32)
            conv_total = conv_total + conv_three[i]
        part[...] = total.astype(BF)
        four[:, rows_at(z, lanes)] = part[...]

        def settle(d, _):
            c3(lax.rem(z + d, deep), z, lax.rem(z + d, deep))[1].wait_send()
            return 0

        lax.fori_loop(1, deep, settle, 0)
        conv_part[...] = conv_total
        to_all(c4, z, deep)

    def step4():
        from_all(c4, z, deep)
        w_out[rows_at(core * groups + dp, blk), :] = four[...]
        tile(conv_out, dp, core * conv_half)[...] = conv_part[...]
        to_all(c5, dp, groups)

    def step5():
        from_all(c5, dp, groups)
        for copy in c6(core):
            copy.start()

    def step6():
        for copy in c6(1 - core):
            copy.wait_recv()
        for copy in c6(core):
            copy.wait_send()

        def settle_dp(d, _):
            peer = lax.rem(dp + d, groups)
            for copy in (*c2(peer, dp, peer), *c5(peer, dp, peer)):
                copy.wait_send()
            return 0

        lax.fori_loop(1, groups, settle_dp, 0)

        def settle_z(d, _):
            peer = lax.rem(z + d, deep)
            for copy in (c3(peer, z, peer)[0], *c4(peer, z, peer)):
                copy.wait_send()
            return 0

        lax.fori_loop(1, deep, settle_z, 0)

    return step1, step2, step3, step4, step5, step6


def reducer_bufs(width, n, groups):
    half, deep = width // 2, n // 2
    blk, lanes = half // groups, width // deep
    conv_lanes = width // (groups // 2)
    dma = pltpu.SemaphoreType.DMA
    bufs = [
        pltpu.VMEM((groups, blk, width), BF),
        pltpu.VMEM((blk, width), BF),
        pltpu.VMEM((deep, blk, lanes), BF),
        pltpu.VMEM((blk, lanes), BF),
        pltpu.VMEM((blk, width), BF),
        pltpu.VMEM((groups, 8, conv_lanes), F32),
        pltpu.VMEM((deep, 8, conv_lanes), F32),
        pltpu.VMEM((8, conv_lanes), F32),
    ]
    sems = [dma((2, groups))] * 2 + [dma((2, deep))] * 2 + [dma((deep,))] * 2
    sems += [dma((2, groups))] * 2 + [dma((2,))] * 2
    return bufs, sems


def local(query_proj, key_proj, value_proj, cotangent, out_weight, conv_weight, rec_starts):
    rows, width = query_proj.shape[1:]
    factor = (lax.axis_size("dp") * lax.axis_size("seq") * rows) ** -0.5
    out, kv, q, weight_sum, conv_sum = layer(
        rec_starts, query_proj[0], key_proj[0], value_proj[0], out_weight, cotangent[0], conv_weight
    )
    out, dq, dk, dv, weight_grad, conv_grad = finish(kv, q, out, weight_sum, conv_sum, factor)
    return out[None], dq[None], dk[None], dv[None], weight_grad, conv_grad


def solution(mesh):
    frames = P("dp", "seq", None)
    return jax.shard_map(
        local,
        mesh=mesh,
        in_specs=(frames, frames, frames, frames, P(), P(), P("dp", None)),
        out_specs=(frames, frames, frames, frames, P(), P()),
        check_vma=False,
    )
```
